512 devices in a mesh: wide: 64 (over z, y_hi, core), narrow: 8 (over x, y_lo).
Axes of the slice: x: 4, y: 8 (y_hi: 4, y_lo: 2; y = y_hi * 2 + y_lo), z: 8, core: 2. Of those that a mesh axis runs over, the one named last changes fastest.
Arguments:
- positions: float32 [3, 131072], P(None, ('wide', 'narrow')), may hold values from 0 to 1
- volumes: float32 [131072], P(('wide', 'narrow')), may hold values from 0.5 to 2
- phase_field: float32 [131072], P(('wide', 'narrow')), may hold values from -1 to 1.4
- stencil_weights: float32 [64, 131072], P(None, ('wide', 'narrow')), may hold values from 0.005 to 0.05
- stencil_slots: int32 [64, 131072], P(None, ('wide', 'narrow')), may hold values from 0 to 767, as said below
- send_lists: int32 [2, 131072], P(None, ('wide', 'narrow')), may hold values from 0 to 255, as said below
Outputs:
- phase_next: float32 [131072], P(('wide', 'narrow'))
- potential_next: float32 [131072], P(('wide', 'narrow'))
The draws below stay inside these ranges and needn't reach their ends.
Inputs may be any that keep to these rules, and one draw needn't show every extreme that they name: `stencil_slots`: entry k of point i names a neighbour in ext of i's block: values below 256 are rows of the same block other than i; 256 + s is slot s of the list that the block one lower along wide (cyclically) sends up, 512 + s slot s of the list that the block one higher sends down; s is always below that list's count c, and every slot below c is named by some point of the receiving block. `send_lists`: each block's list in each row has a count c of 1 to 256: its first c slots hold distinct rows of 0 to 255 and the rest hold 0; in each row some block's list is full.
All inputs are finite; a program needn't handle non-finite values.
Results may differ from the reference program's by a relative error of at most 0.00002.
Values sent between devices are 32-bit elements; how exact they have to be, the bound alone decides.
A program may use at most 64 MiB of HBM per device.

```python
import math
import jax
import jax.numpy as jnp
from jax import lax

PTS_DEV = 256
NEIGHBOURS = 64
SEND_ROWS = 256
POINTS = 131072
N_WIDE = 64
N_NARROW = 8
DEVICES = 512


def plan_counts(key):
    base_key = jax.random.fold_in(key, 7101)
    key_count, key_heavy, key_forced = jax.random.split(base_key, 3)
    counts = jax.random.randint(key_count, (DEVICES, 2), max(SEND_ROWS // 8, 1), SEND_ROWS // 2 + 1)
    heavy = jax.random.randint(key_heavy, (DEVICES, 2), 0, 8) == 0
    forced = jax.random.randint(key_forced, (), 0, DEVICES)
    forced_mask = (jnp.arange(DEVICES) == forced)[:, None]
    return jnp.where(heavy | forced_mask, SEND_ROWS, counts).astype(jnp.int32)


def pick_rows(key_one):
    order = jax.random.permutation(key_one, PTS_DEV)[:SEND_ROWS]
    first = order[0]
    order = jnp.where(order == PTS_DEV - 1, first, order)
    return order.at[0].set(PTS_DEV - 1)


def draw_send_lists(key, part):
    counts = plan_counts(key)
    keys_all = jax.random.split(jax.random.fold_in(key, 7202), DEVICES * 2)
    shuffled = jax.vmap(pick_rows)(keys_all)
    shuffled = shuffled.reshape(DEVICES, 2, SEND_ROWS)
    slot_ids = jnp.arange(SEND_ROWS)
    listed = jnp.where(slot_ids[None, None, :] < counts[:, :, None], shuffled, 0)
    return jnp.transpose(listed, (1, 0, 2)).reshape(2, DEVICES * SEND_ROWS).astype(jnp.int32)


def draw_stencil_slots(key, part):
    counts = plan_counts(key).reshape(N_WIDE, N_NARROW, 2)
    low_count = jnp.roll(counts[:, :, 0], 1, axis=0).reshape(DEVICES, 1, 1)
    high_count = jnp.roll(counts[:, :, 1], -1, axis=0).reshape(DEVICES, 1, 1)
    key_kind, key_raw = jax.random.split(jax.random.fold_in(key, 7303), 2)
    category = jax.random.randint(key_kind, (DEVICES, NEIGHBOURS, PTS_DEV), 0, 4)
    raw_draw = jax.random.randint(key_raw, (DEVICES, NEIGHBOURS, PTS_DEV), 0, 1 << 20)
    row_ids = jnp.arange(PTS_DEV)[None, None, :]
    layer_ids = jnp.arange(NEIGHBOURS)[None, :, None]
    category = jnp.where(layer_ids == 0, 0, jnp.where(layer_ids == 1, 1, category))
    low_slot = jnp.where(layer_ids == 0, row_ids % low_count, raw_draw % low_count)
    high_slot = jnp.where(layer_ids == 1, row_ids % high_count, raw_draw % high_count)
    own_rows = (row_ids + 1 + raw_draw % (PTS_DEV - 1)) % PTS_DEV
    slots_all = jnp.where(category == 0, PTS_DEV + low_slot, jnp.where(category == 1, PTS_DEV + SEND_ROWS + high_slot, own_rows))
    return jnp.transpose(slots_all, (1, 0, 2)).reshape(NEIGHBOURS, POINTS).astype(jnp.int32)


def level_of(own_key, dims, cuts, low, top_value):
    gain, own = 1.0, jax.random.fold_in(own_key, 6)
    for axis_at, shards_of in cuts:
        draws = jnp.exp(jax.random.uniform(jax.random.fold_in(own, axis_at), (shards_of,), jnp.float32, low / len(cuts), top_value / len(cuts)))
        gain = gain * jnp.repeat(draws, dims[axis_at] // shards_of).reshape([-1 if axis == axis_at else 1 for axis in range(len(dims))])
    return gain


def setup_inputs(seed: int = 0) -> dict:
    splits = jax.random.split(jax.random.key(seed), 7)
    return {
        "positions": jnp.clip(1.0 * jax.random.uniform(splits[0], (3, POINTS), jnp.float32) ** level_of(splits[0], (3, POINTS), ((1, 512),), -0.2, 0.2), 0.0, 1.0),
        "volumes": jnp.clip(jnp.exp(math.log(2.0) - 1.3862944 * jax.random.uniform(splits[1], (POINTS,), jnp.float32) ** level_of(splits[1], (POINTS,), ((0, 512),), -0.2, 0.2)), 0.5, 2.0),
        "phase_field": jnp.clip(-1.0 + 2.4 * jax.random.uniform(splits[2], (POINTS,), jnp.float32) ** level_of(splits[2], (POINTS,), ((0, 512),), -0.2, 0.2), -1.0, 1.4),
        "stencil_weights": jnp.clip(jnp.exp(math.log(0.05) - 2.3025851 * jax.random.uniform(splits[3], (NEIGHBOURS, POINTS), jnp.float32) ** level_of(splits[3], (NEIGHBOURS, POINTS), ((1, 512),), -0.2, 0.2)), 0.005, 0.05),
        "stencil_slots": draw_stencil_slots(jax.random.fold_in(splits[6], 71), 0),
        "send_lists": draw_send_lists(jax.random.fold_in(splits[6], 71), 0),
    }


kernel_strength = 0.1
gradient_energy = 0.5
time_step = 0.2


def extend_blocks(field_now, send_lists):
    blocks = field_now.reshape(N_WIDE, N_NARROW, PTS_DEV)
    send_blocks = send_lists.reshape(2, N_WIDE, N_NARROW, SEND_ROWS)
    upward = jnp.take_along_axis(blocks, send_blocks[0], axis=2)
    downward = jnp.take_along_axis(blocks, send_blocks[1], axis=2)
    return jnp.concatenate([blocks, jnp.roll(upward, 1, axis=0), jnp.roll(downward, -1, axis=0)], axis=2)


def laplace(field_now, stencil_weights, stencil_slots, send_lists):
    extended = extend_blocks(field_now, send_lists)
    slot_blocks = stencil_slots.reshape(NEIGHBOURS, N_WIDE, N_NARROW, PTS_DEV)
    neighbour_vals = jax.vmap(lambda slot_layer: jnp.take_along_axis(extended, slot_layer, axis=2))(slot_blocks)
    weight_blocks = stencil_weights.reshape(NEIGHBOURS, N_WIDE, N_NARROW, PTS_DEV)
    blocks = field_now.reshape(N_WIDE, N_NARROW, PTS_DEV)
    return jnp.sum(weight_blocks * (neighbour_vals - blocks[None]), axis=0).reshape(-1)


def kernel_terms(positions, volumes, field_now):
    patch_len = PTS_DEV * N_NARROW
    kernel_decay = 0.5 * float(patch_len) ** (2.0 / 3.0)
    source_all = positions.reshape(3, N_WIDE, patch_len).transpose(1, 0, 2)
    volume_all = volumes.reshape(N_WIDE, patch_len)
    field_all = field_now.reshape(N_WIDE, patch_len)
    targets = positions.reshape(3, N_WIDE, N_NARROW, PTS_DEV).transpose(1, 2, 0, 3)

    def per_patch(operands):
        target_rows, sources, vols, values = operands

        def per_block(target_block):
            distance = (target_block[0][:, None] - sources[0][None, :]) ** 2
            distance = distance + (target_block[1][:, None] - sources[1][None, :]) ** 2
            distance = distance + (target_block[2][:, None] - sources[2][None, :]) ** 2
            gauss_vol = jnp.exp(-kernel_decay * distance) * vols[None, :]
            return jnp.sum(gauss_vol, axis=1), jnp.sum(gauss_vol * values[None, :], axis=1)

        return lax.map(per_block, target_rows)

    sums_mass, sums_field = lax.map(per_patch, (targets, source_all, volume_all, field_all))
    return (kernel_strength * sums_mass).reshape(-1), (kernel_strength * sums_field).reshape(-1)


def potential(field_now, positions, volumes, stencil_weights, stencil_slots, send_lists):
    amass, smooth = kernel_terms(positions, volumes, field_now)
    kernel_term = amass * field_now - smooth
    lap_term = laplace(field_now, stencil_weights, stencil_slots, send_lists)
    return field_now ** 3 - field_now + kernel_term - gradient_energy * lap_term


def reference(positions, volumes, phase_field, stencil_weights, stencil_slots, send_lists):
    potential_now = potential(phase_field, positions, volumes, stencil_weights, stencil_slots, send_lists)
    phase_next = phase_field + time_step * laplace(potential_now, stencil_weights, stencil_slots, send_lists)
    potential_next = potential(phase_next, positions, volumes, stencil_weights, stencil_slots, send_lists)
    return phase_next, potential_next
```

```python
import functools
import jax
import jax.numpy as jnp
from jax import lax
from jax.experimental import pallas as pl
from jax.experimental.pallas import tpu as pltpu
from jax.sharding import PartitionSpec as P

kernel_strength = 0.1
gradient_energy = 0.5
time_step = 0.2

LANES = 128
MESH = pl.DeviceIdType.MESH
PEERS = ((0, 1), (1, 0), (3, 0), (1, 1), (3, 1), (2, 0), (2, 1))
CHUNK = 64


def halves(row):
    return row[:, :LANES], row[:, LANES:]


def lookup(row, lanes):
    return jnp.take_along_axis(
        jnp.broadcast_to(row, lanes.shape), lanes, axis=1, mode="promise_in_bounds"
    )


def step_kernel(
    n_wide, kernel_decay,
    pos_h, vol_h, field_h, weight_h, slot_h, list_h,
    next_o, pot_o,
    pos_v, vol_v, field_v, weight_v, slot_v, list_v,
    pack_s, pack_r, column, gauss, mass_acc, field_acc, masked, lane_of, pick,
    halo_s, halo_r, next_s, next_r,
    load_sem, pack_ss, pack_rs, halo_ss, halo_rs, next_ss, next_rs,
):
    wide = lax.axis_index("wide")
    narrow = lax.axis_index("narrow")
    x_at, y_at = narrow // 2, narrow % 2
    peers = [
        (wide, lax.rem(x_at + dx, 4) * 2 + lax.rem(y_at + dy, 2)) for dx, dy in PEERS
    ]
    up = (lax.rem(wide + 1, n_wide), narrow)
    down = (lax.rem(wide + n_wide - 1, n_wide), narrow)

    barrier = pltpu.get_barrier_semaphore()
    for target in (up, down, *reversed(peers)):
        pl.semaphore_signal(barrier, inc=1, device_id=target, device_id_type=MESH)

    loads = [
        pltpu.make_async_copy(src, dst, load_sem.at[i])
        for i, (src, dst) in enumerate(
            (
                (list_h, list_v), (field_h, field_v), (pos_h, pos_v), (vol_h, vol_v),
                (slot_h, slot_v), (weight_h, weight_v),
            )
        )
    ]
    for load in loads:
        load.start()

    def to_halo(rows, turn):
        low, high = halves(rows)
        pairs = pick[...]
        lanes = pairs & (LANES - 1)
        values = jnp.where(pairs >= LANES, lookup(high, lanes), lookup(low, lanes))
        halo_s[turn] = values[:4]

    def halo_copies(turn):
        return [
            pltpu.make_async_remote_copy(
                src_ref=halo_s.at[turn],
                dst_ref=halo_r.at[turn, side],
                send_sem=halo_ss.at[turn, side],
                recv_sem=halo_rs.at[turn, side],
                device_id=target,
                device_id_type=MESH,
            )
            for side, target in enumerate((up, down))
        ]

    def lap_part(rows, first, field_row):
        field_halves = halves(field_row)
        parts = []
        for at in range(2):
            lanes = lane_of[:, at * LANES:(at + 1) * LANES]
            total = None
            for h, row in enumerate(rows):
                weights = masked[first + h, :, at * LANES:(at + 1) * LANES]
                term = weights * (lookup(row, lanes) - field_halves[at])
                total = term if total is None else total + term
            parts.append(jnp.sum(total.reshape(8, 8, LANES), axis=0))
        return parts

    def halo_rows(turn, side):
        base = 2 * side
        return (
            halo_r[turn, side, base:base + 1, :],
            halo_r[turn, side, base + 1:base + 2, :],
        )

    def finish_lap(parts):
        return jnp.concatenate(
            [jnp.sum(part, axis=0, keepdims=True) for part in parts], axis=1
        )

    def lap_rest(parts, turn, field_row):
        copies = halo_copies(turn)
        for side in range(2):
            copies[side].wait_recv()
            more = lap_part(halo_rows(turn, side), 2 + 2 * side, field_row)
            parts = [a + b for a, b in zip(parts, more)]
        return finish_lap(parts)

    def add_sources(slot, source):
        rows = [source[r] for r in range(5)]
        for at in range(2):
            sx, sy, sz, sv, sf = [
                row[:, at * LANES:(at + 1) * LANES] for row in rows
            ]
            for t in range(0, 256, CHUNK):
                span = slice(t, t + CHUNK)
                distance = (column[0, span] - sx) ** 2
                distance = distance + (column[1, span] - sy) ** 2
                distance = distance + (column[2, span] - sz) ** 2
                value = jnp.exp(-kernel_decay * distance) * sv
                gauss[slot, at, span] = value
                if slot == 7 and at == 0:
                    mass_acc[span] = value
                    field_acc[span] = value * sf
                else:
                    mass_acc[span] += value
                    field_acc[span] += value * sf

    def add_field(slot, row):
        for at, part in enumerate(halves(row)):
            for t in range(0, 256, CHUNK):
                span = slice(t, t + CHUNK)
                value = gauss[slot, at, span] * part
                if slot == 7 and at == 0:
                    field_acc[span] = value
                else:
                    field_acc[span] += value

    def to_row(acc):
        return jnp.concatenate(
            [
                jnp.sum(acc[at * LANES:(at + 1) * LANES].T, axis=0, keepdims=True)
                for at in range(2)
            ],
            axis=1,
        )

    def potential(rows, mass, smooth, lap):
        kernel_term = mass * rows - kernel_strength * smooth
        return rows * rows * rows - rows + kernel_term - gradient_energy * lap

    loads[0].wait()
    loads[1].wait()
    for r in range(2):
        for at in range(2):
            pick[2 * r + at:2 * r + at + 1] = list_v[r:r + 1, at * LANES:(at + 1) * LANES]
    pick[4:8] = jnp.zeros((4, LANES), jnp.int32)
    field = field_v[...]
    to_halo(field, 0)
    loads[2].wait()
    loads[3].wait()
    for r in range(3):
        pack_s[r] = pos_v[r:r + 1]
    pack_s[3] = vol_v[...]
    pack_s[4] = field

    pl.semaphore_wait(barrier, 2 + len(peers))

    pack_copies = [
        pltpu.make_async_remote_copy(
            src_ref=pack_s,
            dst_ref=pack_r.at[i],
            send_sem=pack_ss.at[i],
            recv_sem=pack_rs.at[i],
            device_id=target,
            device_id_type=MESH,
        )
        for i, target in enumerate(peers)
    ]
    next_copies = [
        pltpu.make_async_remote_copy(
            src_ref=next_s,
            dst_ref=next_r.at[i],
            send_sem=next_ss.at[i],
            recv_sem=next_rs.at[i],
            device_id=target,
            device_id_type=MESH,
        )
        for i, target in enumerate(peers)
    ]
    for copy in halo_copies(0):
        copy.start()
    for copy in reversed(pack_copies):
        copy.start()

    for r in range(3):
        for at, part in enumerate(halves(pos_v[r:r + 1])):
            column[r, at * LANES:(at + 1) * LANES] = jnp.broadcast_to(part, (LANES, LANES)).T
    loads[4].wait()
    loads[5].wait()
    slots = slot_v[...]
    lane_of[...] = slots & (LANES - 1)
    rows_of = slots >> 7
    weights = weight_v[...]
    for h in range(6):
        masked[h] = jnp.where(rows_of == h, weights, 0.0)
    lap_now = lap_part(halves(field), 0, field)
    add_sources(7, pack_s)
    for i, copy in enumerate(pack_copies):
        copy.wait_recv()
        add_sources(i, pack_r.at[i])
    mass = kernel_strength * to_row(mass_acc[...])
    smooth = to_row(field_acc[...])
    lap = lap_rest(lap_now, 0, field)
    now = potential(field, mass, smooth, lap)

    to_halo(now, 1)
    for copy in halo_copies(1):
        copy.start()
    lap = lap_rest(lap_part(halves(now), 0, now), 1, now)
    after = field + time_step * lap

    next_s[...] = after
    to_halo(after, 2)
    for copy in halo_copies(2):
        copy.start()
    for copy in reversed(next_copies):
        copy.start()
    next_o[...] = after
    lap_own = lap_part(halves(after), 0, after)
    add_field(7, after)
    for i, copy in enumerate(next_copies):
        copy.wait_recv()
        add_field(i, next_r[i])
    smooth = to_row(field_acc[...])
    lap = lap_rest(lap_own, 2, after)
    pot_o[...] = potential(after, mass, smooth, lap)

    for copy in pack_copies + next_copies:
        copy.wait_send()
    for turn in range(3):
        for copy in halo_copies(turn):
            copy.wait_send()


def shards(n_wide, positions, volumes, phase_field, stencil_weights, stencil_slots, send_lists):
    own = phase_field.shape[0]
    patch_len = own * lax.axis_size("narrow")
    kernel_decay = 0.5 * float(patch_len) ** (2.0 / 3.0)
    row = jax.ShapeDtypeStruct((1, own), jnp.float32)
    in_hbm = pl.BlockSpec(memory_space=pl.ANY)
    in_vmem = pl.BlockSpec(memory_space=pltpu.VMEM)
    f32 = jnp.float32
    n_peers = len(PEERS)
    after, pot = pl.pallas_call(
        functools.partial(step_kernel, n_wide, kernel_decay),
        out_shape=(row, row),
        in_specs=[in_hbm] * 6,
        out_specs=(in_vmem, in_vmem),
        scratch_shapes=[
            pltpu.VMEM((3, own), f32),
            pltpu.VMEM((1, own), f32),
            pltpu.VMEM((1, own), f32),
            pltpu.VMEM(stencil_weights.shape, f32),
            pltpu.VMEM(stencil_slots.shape, jnp.int32),
            pltpu.VMEM((2, own), jnp.int32),
            pltpu.VMEM((5, 1, own), f32),
            pltpu.VMEM((n_peers, 5, 1, own), f32),
            pltpu.VMEM((3, own, LANES), f32),
            pltpu.VMEM((n_peers + 1, 2, own, LANES), f32),
            pltpu.VMEM((own, LANES), f32),
            pltpu.VMEM((own, LANES), f32),
            pltpu.VMEM((6, *stencil_weights.shape), f32),
            pltpu.VMEM(stencil_slots.shape, jnp.int32),
            pltpu.VMEM((8, LANES), jnp.int32),
            pltpu.VMEM((3, 4, LANES), f32),
            pltpu.VMEM((3, 2, 4, LANES), f32),
            pltpu.VMEM((1, own), f32),
            pltpu.VMEM((n_peers, 1, own), f32),
            pltpu.SemaphoreType.DMA((6,)),
            pltpu.SemaphoreType.DMA((n_peers,)),
            pltpu.SemaphoreType.DMA((n_peers,)),
            pltpu.SemaphoreType.DMA((3, 2)),
            pltpu.SemaphoreType.DMA((3, 2)),
            pltpu.SemaphoreType.DMA((n_peers,)),
            pltpu.SemaphoreType.DMA((n_peers,)),
        ],
        compiler_params=pltpu.CompilerParams(collective_id=0, has_side_effects=True),
    )(
        positions,
        volumes.reshape(1, own),
        phase_field.reshape(1, own),
        stencil_weights,
        stencil_slots,
        send_lists,
    )
    return after.reshape(own), pot.reshape(own)


def solution(mesh):
    placed = (
        P(None, ("wide", "narrow")),
        P(("wide", "narrow")),
        P(("wide", "narrow")),
        P(None, ("wide", "narrow")),
        P(None, ("wide", "narrow")),
        P(None, ("wide", "narrow")),
    )
    return jax.shard_map(
        functools.partial(shards, mesh.shape["wide"]),
        mesh=mesh,
        in_specs=placed,
        out_specs=(P(("wide", "narrow")), P(("wide", "narrow"))),
        check_vma=False,
    )
```

```python
import functools
import jax
import jax.numpy as jnp
from jax import lax
from jax.experimental import pallas as pl
from jax.experimental.pallas import tpu as pltpu
from jax.sharding import PartitionSpec as P

kernel_strength = 0.1
gradient_energy = 0.5
time_step = 0.2

LANES = 128
MESH = pl.DeviceIdType.MESH
PEERS = ((0, 1), (1, 0), (3, 0), (1, 1), (3, 1), (2, 0), (2, 1))
CHUNK = 64


def halves(row):
    return row[:, :LANES], row[:, LANES:]


def lookup(row, lanes):
    return jnp.take_along_axis(
        jnp.broadcast_to(row, lanes.shape), lanes, axis=1, mode="promise_in_bounds"
    )


def step_kernel(
    n_wide, kernel_decay,
    pos_h, vol_h, field_h, weight_h, slot_h, list_h,
    out_o,
    pos_v, vol_v, field_v, weight_v, slot_v, list_v,
    pack_s, pack_r, column, gauss, mass_acc, field_acc, masked, lane_of, pick,
    halo_s, halo_r, next_s, next_r,
    load_sem, pack_ss, pack_rs, halo_ss, halo_rs, next_ss, next_rs,
):
    wide = lax.axis_index("wide")
    narrow = lax.axis_index("narrow")
    x_at, y_at = narrow // 2, narrow % 2
    peers = [
        (wide, lax.rem(x_at + dx, 4) * 2 + lax.rem(y_at + dy, 2)) for dx, dy in PEERS
    ]
    up = (lax.rem(wide + 1, n_wide), narrow)
    down = (lax.rem(wide + n_wide - 1, n_wide), narrow)

    barrier = pltpu.get_barrier_semaphore()
    for target in (up, down, *reversed(peers)):
        pl.semaphore_signal(barrier, inc=1, device_id=target, device_id_type=MESH)

    loads = [
        pltpu.make_async_copy(src, dst, load_sem.at[i])
        for i, (src, dst) in enumerate(
            (
                (list_h, list_v), (field_h, field_v), (pos_h, pos_v), (vol_h, vol_v),
                (slot_h, slot_v), (weight_h, weight_v),
            )
        )
    ]
    for load in loads:
        load.start()

    def to_halo(rows, turn):
        low, high = halves(rows)
        pairs = pick[...]
        lanes = pairs & (LANES - 1)
        values = jnp.where(pairs >= LANES, lookup(high, lanes), lookup(low, lanes))
        halo_s[turn] = values[:4]

    def halo_copies(turn):
        return [
            pltpu.make_async_remote_copy(
                src_ref=halo_s.at[turn],
                dst_ref=halo_r.at[turn, side],
                send_sem=halo_ss.at[turn, side],
                recv_sem=halo_rs.at[turn, side],
                device_id=target,
                device_id_type=MESH,
            )
            for side, target in enumerate((up, down))
        ]

    def lap_part(rows, first, field_row):
        field_halves = halves(field_row)
        parts = []
        for at in range(2):
            lanes = lane_of[:, at * LANES:(at + 1) * LANES]
            total = None
            for h, row in enumerate(rows):
                weights = masked[first + h, :, at * LANES:(at + 1) * LANES]
                term = weights * (lookup(row, lanes) - field_halves[at])
                total = term if total is None else total + term
            parts.append(jnp.sum(total.reshape(8, 8, LANES), axis=0))
        return parts

    def halo_rows(turn, side):
        base = 2 * side
        return (
            halo_r[turn, side, base:base + 1, :],
            halo_r[turn, side, base + 1:base + 2, :],
        )

    def finish_lap(parts):
        return jnp.concatenate(
            [jnp.sum(part, axis=0, keepdims=True) for part in parts], axis=1
        )

    def lap_rest(parts, turn, field_row):
        copies = halo_copies(turn)
        for side in range(2):
            copies[side].wait_recv()
            more = lap_part(halo_rows(turn, side), 2 + 2 * side, field_row)
            parts = [a + b for a, b in zip(parts, more)]
        return finish_lap(parts)

    def add_sources(slot, source):
        rows = [source[r] for r in range(5)]
        for at in range(2):
            sx, sy, sz, sv, sf = [
                row[:, at * LANES:(at + 1) * LANES] for row in rows
            ]
            for t in range(0, 256, CHUNK):
                span = slice(t, t + CHUNK)
                distance = (column[0, span] - sx) ** 2
                distance = distance + (column[1, span] - sy) ** 2
                distance = distance + (column[2, span] - sz) ** 2
                value = jnp.exp(-kernel_decay * distance) * sv
                gauss[slot, at, span] = value
                if slot == 7 and at == 0:
                    mass_acc[span] = value
                    field_acc[span] = value * sf
                else:
                    mass_acc[span] += value
                    field_acc[span] += value * sf

    def add_field(slot, row):
        for at, part in enumerate(halves(row)):
            for t in range(0, 256, CHUNK):
                span = slice(t, t + CHUNK)
                value = gauss[slot, at, span] * part
                if slot == 7 and at == 0:
                    field_acc[span] = value
                else:
                    field_acc[span] += value

    def to_row(acc):
        return jnp.concatenate(
            [
                jnp.sum(acc[at * LANES:(at + 1) * LANES].T, axis=0, keepdims=True)
                for at in range(2)
            ],
            axis=1,
        )

    def potential(rows, mass, smooth, lap):
        kernel_term = mass * rows - kernel_strength * smooth
        return rows * rows * rows - rows + kernel_term - gradient_energy * lap

    loads[0].wait()
    loads[1].wait()
    for r in range(2):
        for at in range(2):
            pick[2 * r + at:2 * r + at + 1] = list_v[r:r + 1, at * LANES:(at + 1) * LANES]
    pick[4:8] = jnp.zeros((4, LANES), jnp.int32)
    field = field_v[...]
    to_halo(field, 0)
    loads[2].wait()
    loads[3].wait()
    for r in range(3):
        pack_s[r] = pos_v[r:r + 1]
    pack_s[3] = vol_v[...]
    pack_s[4] = field

    pl.semaphore_wait(barrier, 2 + len(peers))

    pack_copies = [
        pltpu.make_async_remote_copy(
            src_ref=pack_s,
            dst_ref=pack_r.at[i],
            send_sem=pack_ss.at[i],
            recv_sem=pack_rs.at[i],
            device_id=target,
            device_id_type=MESH,
        )
        for i, target in enumerate(peers)
    ]
    next_copies = [
        pltpu.make_async_remote_copy(
            src_ref=next_s,
            dst_ref=next_r.at[i],
            send_sem=next_ss.at[i],
            recv_sem=next_rs.at[i],
            device_id=target,
            device_id_type=MESH,
        )
        for i, target in enumerate(peers)
    ]
    for copy in halo_copies(0):
        copy.start()
    for copy in reversed(pack_copies):
        copy.start()

    for r in range(3):
        for at, part in enumerate(halves(pos_v[r:r + 1])):
            column[r, at * LANES:(at + 1) * LANES] = jnp.broadcast_to(part, (LANES, LANES)).T
    loads[4].wait()
    loads[5].wait()
    slots = slot_v[...]
    lane_of[...] = slots & (LANES - 1)
    rows_of = slots >> 7
    weights = weight_v[...]
    for h in range(6):
        masked[h] = jnp.where(rows_of == h, weights, 0.0)
    lap_now = lap_part(halves(field), 0, field)
    add_sources(7, pack_s)
    for i, copy in enumerate(pack_copies):
        copy.wait_recv()
        add_sources(i, pack_r.at[i])
    mass = kernel_strength * to_row(mass_acc[...])
    smooth = to_row(field_acc[...])
    lap = lap_rest(lap_now, 0, field)
    now = potential(field, mass, smooth, lap)

    to_halo(now, 1)
    for copy in halo_copies(1):
        copy.start()
    lap = lap_rest(lap_part(halves(now), 0, now), 1, now)
    after = field + time_step * lap

    next_s[...] = after
    to_halo(after, 2)
    for copy in halo_copies(2):
        copy.start()
    for copy in reversed(next_copies):
        copy.start()
    out_o[0] = after
    lap_own = lap_part(halves(after), 0, after)
    add_field(7, after)
    for i, copy in enumerate(next_copies):
        copy.wait_recv()
        add_field(i, next_r[i])
    smooth = to_row(field_acc[...])
    lap = lap_rest(lap_own, 2, after)
    out_o[1] = potential(after, mass, smooth, lap)

    for copy in pack_copies + next_copies:
        copy.wait_send()
    for turn in range(3):
        for copy in halo_copies(turn):
            copy.wait_send()


def shards(n_wide, positions, volumes, phase_field, stencil_weights, stencil_slots, send_lists):
    own = phase_field.shape[0]
    patch_len = own * lax.axis_size("narrow")
    kernel_decay = 0.5 * float(patch_len) ** (2.0 / 3.0)
    in_hbm = pl.BlockSpec(memory_space=pltpu.HBM)
    in_vmem = pl.BlockSpec(memory_space=pltpu.VMEM)
    f32 = jnp.float32
    n_peers = len(PEERS)
    both = pl.pallas_call(
        functools.partial(step_kernel, n_wide, kernel_decay),
        out_shape=jax.ShapeDtypeStruct((2, 1, own), f32),
        in_specs=[in_hbm] * 6,
        out_specs=in_vmem,
        scratch_shapes=[
            pltpu.VMEM((3, own), f32),
            pltpu.VMEM((1, own), f32),
            pltpu.VMEM((1, own), f32),
            pltpu.VMEM(stencil_weights.shape, f32),
            pltpu.VMEM(stencil_slots.shape, jnp.int32),
            pltpu.VMEM((2, own), jnp.int32),
            pltpu.VMEM((5, 1, own), f32),
            pltpu.VMEM((n_peers, 5, 1, own), f32),
            pltpu.VMEM((3, own, LANES), f32),
            pltpu.VMEM((n_peers + 1, 2, own, LANES), f32),
            pltpu.VMEM((own, LANES), f32),
            pltpu.VMEM((own, LANES), f32),
            pltpu.VMEM((6, *stencil_weights.shape), f32),
            pltpu.VMEM(stencil_slots.shape, jnp.int32),
            pltpu.VMEM((8, LANES), jnp.int32),
            pltpu.VMEM((3, 4, LANES), f32),
            pltpu.VMEM((3, 2, 4, LANES), f32),
            pltpu.VMEM((1, own), f32),
            pltpu.VMEM((n_peers, 1, own), f32),
            pltpu.SemaphoreType.DMA((6,)),
            pltpu.SemaphoreType.DMA((n_peers,)),
            pltpu.SemaphoreType.DMA((n_peers,)),
            pltpu.SemaphoreType.DMA((3, 2)),
            pltpu.SemaphoreType.DMA((3, 2)),
            pltpu.SemaphoreType.DMA((n_peers,)),
            pltpu.SemaphoreType.DMA((n_peers,)),
        ],
        compiler_params=pltpu.CompilerParams(
            collective_id=0, has_side_effects=True, vmem_limit_bytes=16 * 1024 * 1024
        ),
    )(
        *(
            pltpu.with_memory_space_constraint(array, pltpu.HBM)
            for array in (
                positions,
                volumes.reshape(1, own),
                phase_field.reshape(1, own),
                stencil_weights,
                stencil_slots,
                send_lists,
            )
        )
    )
    both = both.reshape(2 * own)
    return both[:own], both[own:]


def solution(mesh):
    placed = (
        P(None, ("wide", "narrow")),
        P(("wide", "narrow")),
        P(("wide", "narrow")),
        P(None, ("wide", "narrow")),
        P(None, ("wide", "narrow")),
        P(None, ("wide", "narrow")),
    )
    return jax.shard_map(
        functools.partial(shards, mesh.shape["wide"]),
        mesh=mesh,
        in_specs=placed,
        out_specs=(P(("wide", "narrow")), P(("wide", "narrow"))),
        check_vma=False,
    )
```

```python
import functools
import jax
import jax.numpy as jnp
from jax import lax
from jax.experimental import pallas as pl
from jax.experimental.pallas import tpu as pltpu
from jax.sharding import PartitionSpec as P

kernel_strength = 0.1
gradient_energy = 0.5
time_step = 0.2

LANES = 128
MESH = pl.DeviceIdType.MESH
PEERS = ((0, 1), (1, 0), (3, 0), (1, 1), (3, 1), (2, 0), (2, 1))
CHUNK = 64
LOG2_E = 1.4426950408889634


def halves(row):
    return row[:, :LANES], row[:, LANES:]


def lookup(row, lanes):
    return jnp.take_along_axis(
        jnp.broadcast_to(row, lanes.shape), lanes, axis=1, mode="promise_in_bounds"
    )


def join(pair):
    return jnp.concatenate(pair, axis=1)


def step_kernel(
    n_wide, kernel_decay,
    pos_h, vol_h, field_h, weight_h, slot_h, list_h,
    out_o,
    pos_v, vol_v, field_v, weight_v, slot_v, list_v,
    pack_s, pack_r, column, gauss, acc, masked, lane_of, pick,
    halo_s, halo_r, next_s, next_r,
    load_sem, send_sem, pack_rs, halo_rs, next_rs,
):
    wide = lax.axis_index("wide")
    narrow = lax.axis_index("narrow")
    x_at, y_at = narrow // 2, narrow % 2
    peers = [
        (wide, lax.rem(x_at + dx, 4) * 2 + lax.rem(y_at + dy, 2)) for dx, dy in PEERS
    ]
    up = (lax.rem(wide + 1, n_wide), narrow)
    down = (lax.rem(wide + n_wide - 1, n_wide), narrow)
    near_side = 1 - wide % 2
    far_side = 1 - near_side

    barrier = pltpu.get_barrier_semaphore()
    for target in (up, down, *reversed(peers)):
        pl.semaphore_signal(barrier, inc=1, device_id=target, device_id_type=MESH)

    loads = [
        pltpu.make_async_copy(src, dst, load_sem.at[i])
        for i, (src, dst) in enumerate(
            (
                (list_h, list_v), (field_h, field_v), (pos_h, pos_v), (vol_h, vol_v),
                (slot_h, slot_v), (weight_h, weight_v),
            )
        )
    ]
    for load in loads:
        load.start()

    def to_halo(rows, turn):
        low, high = halves(rows)
        pairs = pick[...]
        lanes = pairs & (LANES - 1)
        values = jnp.where(pairs >= LANES, lookup(high, lanes), lookup(low, lanes))
        halo_s[turn] = values[:4]

    def halo_copies(turn):
        return [
            pltpu.make_async_remote_copy(
                src_ref=halo_s.at[turn],
                dst_ref=halo_r.at[turn, side],
                send_sem=send_sem.at[1],
                recv_sem=halo_rs.at[turn, side],
                device_id=target,
                device_id_type=MESH,
            )
            for side, target in enumerate((up, down))
        ]

    def halo_wait(turn, side):
        pltpu.make_async_remote_copy(
            src_ref=halo_s.at[turn],
            dst_ref=halo_r.at[turn, side],
            send_sem=send_sem.at[1],
            recv_sem=halo_rs.at[turn, side],
            device_id=up,
            device_id_type=MESH,
        ).wait_recv()

    def lap_part(rows, first, field_row):
        field_halves = halves(field_row)
        parts = []
        for at in range(2):
            lanes = lane_of[:, at * LANES:(at + 1) * LANES]
            total = None
            for h, row in enumerate(rows):
                weights = masked[first, h, :, at * LANES:(at + 1) * LANES]
                term = weights * (lookup(row, lanes) - field_halves[at])
                total = term if total is None else total + term
            parts.append(jnp.sum(total.reshape(8, 8, LANES), axis=0))
        return parts

    def lap_side(parts, turn, side, field_row):
        halo_wait(turn, side)
        rows = halo_r[turn, side]
        is_high = side == 1
        rows = [jnp.where(is_high, rows[2 + h:3 + h], rows[h:h + 1]) for h in range(2)]
        more = lap_part(rows, 1 + side, field_row)
        return [a + b for a, b in zip(parts, more)]

    def add_sources(slot, source):
        rows = [halves(source[r]) for r in range(5)]
        for t in range(0, 256, CHUNK):
            span = slice(t, t + CHUNK)
            total = None
            for at in range(2):
                sx, sy, sz, sv, sf = [row[at] for row in rows]
                distance = (column[0, span] - sx) ** 2
                distance = distance + (column[1, span] - sy) ** 2
                distance = distance + (column[2, span] - sz) ** 2
                value = jnp.exp2(distance * (-kernel_decay * LOG2_E)) * sv
                gauss[slot, at, span] = value
                term = value * (column[3, span] - sf)
                total = term if total is None else total + term
            if slot == 7:
                acc[span] = total
            else:
                acc[span] += total

    def add_field(slot, row):
        low, high = halves(row)
        for t in range(0, 256, CHUNK):
            span = slice(t, t + CHUNK)
            value = gauss[slot, 0, span] * low + gauss[slot, 1, span] * high
            if slot == 7:
                acc[span] = value
            else:
                acc[span] += value

    def fold(total):
        return [
            jnp.sum(total[at * LANES:(at + 1) * LANES].T.reshape(16, 8, LANES), axis=0)
            for at in range(2)
        ]

    def finish(parts):
        return join([jnp.sum(part, axis=0, keepdims=True) for part in parts])

    loads[0].wait()
    loads[1].wait()
    for r in range(2):
        for at in range(2):
            pick[2 * r + at:2 * r + at + 1] = list_v[r:r + 1, at * LANES:(at + 1) * LANES]
    pick[4:8] = jnp.zeros((4, LANES), jnp.int32)
    field = field_v[...]
    to_halo(field, 0)
    loads[2].wait()
    loads[3].wait()
    for r in range(3):
        pack_s[r] = pos_v[r:r + 1]
    pack_s[3] = vol_v[...]
    pack_s[4] = field

    pl.semaphore_wait(barrier, 2 + len(peers))

    pack_copies = [
        pltpu.make_async_remote_copy(
            src_ref=pack_s,
            dst_ref=pack_r.at[i],
            send_sem=send_sem.at[0],
            recv_sem=pack_rs.at[i],
            device_id=target,
            device_id_type=MESH,
        )
        for i, target in enumerate(peers)
    ]
    next_copies = [
        pltpu.make_async_remote_copy(
            src_ref=next_s,
            dst_ref=next_r.at[i],
            send_sem=send_sem.at[2],
            recv_sem=next_rs.at[i],
            device_id=target,
            device_id_type=MESH,
        )
        for i, target in enumerate(peers)
    ]
    for copy in halo_copies(0):
        copy.start()
    for copy in reversed(pack_copies):
        copy.start()

    for r, row in enumerate((pos_v[0:1], pos_v[1:2], pos_v[2:3], field)):
        for at, part in enumerate(halves(row)):
            column[r, at * LANES:(at + 1) * LANES] = jnp.broadcast_to(part, (LANES, LANES)).T
    add_sources(7, pack_s)
    loads[4].wait()
    loads[5].wait()
    slots = slot_v[...]
    lane_of[...] = slots & (LANES - 1)
    rows_of = slots >> 7
    weights = weight_v[...]
    for h in range(6):
        masked[h // 2, h % 2] = jnp.where(rows_of == h, weights, 0.0)
    lap = lap_part(halves(field), 0, field)
    for i in range(3):
        pack_copies[i].wait_recv()
        add_sources(i, pack_r.at[i])
    lap = lap_side(lap, 0, near_side, field)
    for i in range(3, 6):
        pack_copies[i].wait_recv()
        add_sources(i, pack_r.at[i])
    lap = lap_side(lap, 0, far_side, field)
    pack_copies[6].wait_recv()
    add_sources(6, pack_r.at[6])
    kernel_term = fold(acc[...])
    now = field * field * field - field + finish(
        [kernel_strength * a - gradient_energy * b for a, b in zip(kernel_term, lap)]
    )

    to_halo(now, 1)
    for copy in halo_copies(1):
        copy.start()
    lap = lap_part(halves(now), 0, now)
    lap = lap_side(lap, 1, near_side, now)
    for t in range(0, 256, CHUNK):
        span = slice(t, t + CHUNK)
        total = gauss[0, 0, span] + gauss[0, 1, span]
        for slot in range(1, 8):
            total = total + (gauss[slot, 0, span] + gauss[slot, 1, span])
        acc[span] = total
    mass = finish([kernel_strength * a for a in fold(acc[...])])
    after = field + time_step * finish(lap_side(lap, 1, far_side, now))

    next_s[...] = after
    for copy in reversed(next_copies):
        copy.start()
    to_halo(after, 2)
    for copy in halo_copies(2):
        copy.start()
    out_o[0] = after
    rest = after * after * after - after + mass * after
    lap = lap_part(halves(after), 0, after)
    add_field(7, after)
    for i in range(3):
        next_copies[i].wait_recv()
        add_field(i, next_r[i])
    lap = lap_side(lap, 2, near_side, after)
    for i in range(3, 6):
        next_copies[i].wait_recv()
        add_field(i, next_r[i])
    lap = lap_side(lap, 2, far_side, after)
    next_copies[6].wait_recv()
    add_field(6, next_r[6])
    smooth = fold(acc[...])
    out_o[1] = rest - finish(
        [kernel_strength * a + gradient_energy * b for a, b in zip(smooth, lap)]
    )

    for kind, whole in enumerate((pack_r, halo_r, next_r)):
        pltpu.make_async_copy(whole, whole, send_sem.at[kind]).wait()


def shards(n_wide, positions, volumes, phase_field, stencil_weights, stencil_slots, send_lists):
    own = phase_field.shape[0]
    patch_len = own * lax.axis_size("narrow")
    kernel_decay = 0.5 * float(patch_len) ** (2.0 / 3.0)
    in_hbm = pl.BlockSpec(memory_space=pltpu.HBM)
    in_vmem = pl.BlockSpec(memory_space=pltpu.VMEM)
    f32 = jnp.float32
    n_peers = len(PEERS)
    both = pl.pallas_call(
        functools.partial(step_kernel, n_wide, kernel_decay),
        out_shape=jax.ShapeDtypeStruct((2, 1, own), f32),
        in_specs=[in_hbm] * 6,
        out_specs=in_vmem,
        scratch_shapes=[
            pltpu.VMEM((3, own), f32),
            pltpu.VMEM((1, own), f32),
            pltpu.VMEM((1, own), f32),
            pltpu.VMEM(stencil_weights.shape, f32),
            pltpu.VMEM(stencil_slots.shape, jnp.int32),
            pltpu.VMEM((2, own), jnp.int32),
            pltpu.VMEM((5, 1, own), f32),
            pltpu.VMEM((n_peers, 5, 1, own), f32),
            pltpu.VMEM((4, own, LANES), f32),
            pltpu.VMEM((n_peers + 1, 2, own, LANES), f32),
            pltpu.VMEM((own, LANES), f32),
            pltpu.VMEM((3, 2, *stencil_weights.shape), f32),
            pltpu.VMEM(stencil_slots.shape, jnp.int32),
            pltpu.VMEM((8, LANES), jnp.int32),
            pltpu.VMEM((3, 4, LANES), f32),
            pltpu.VMEM((3, 2, 4, LANES), f32),
            pltpu.VMEM((1, own), f32),
            pltpu.VMEM((n_peers, 1, own), f32),
            pltpu.SemaphoreType.DMA((6,)),
            pltpu.SemaphoreType.DMA((3,)),
            pltpu.SemaphoreType.DMA((n_peers,)),
            pltpu.SemaphoreType.DMA((3, 2)),
            pltpu.SemaphoreType.DMA((n_peers,)),
        ],
        compiler_params=pltpu.CompilerParams(
            collective_id=0, has_side_effects=True, vmem_limit_bytes=16 * 1024 * 1024
        ),
    )(
        *(
            pltpu.with_memory_space_constraint(array, pltpu.HBM)
            for array in (
                positions,
                volumes.reshape(1, own),
                phase_field.reshape(1, own),
                stencil_weights,
                stencil_slots,
                send_lists,
            )
        )
    )
    both = both.reshape(2 * own)
    return both[:own], both[own:]


def solution(mesh):
    placed = (
        P(None, ("wide", "narrow")),
        P(("wide", "narrow")),
        P(("wide", "narrow")),
        P(None, ("wide", "narrow")),
        P(None, ("wide", "narrow")),
        P(None, ("wide", "narrow")),
    )
    return jax.shard_map(
        functools.partial(shards, mesh.shape["wide"]),
        mesh=mesh,
        in_specs=placed,
        out_specs=(P(("wide", "narrow")), P(("wide", "narrow"))),
        check_vma=False,
    )
```

```python
import functools
import jax
import jax.numpy as jnp
from jax import lax
from jax.experimental import pallas as pl
from jax.experimental.pallas import tpu as pltpu
from jax.sharding import PartitionSpec as P

kernel_strength = 0.1
gradient_energy = 0.5
time_step = 0.2

LANES = 128
MESH = pl.DeviceIdType.MESH
PEERS = ((0, 1), (1, 0), (3, 0), (1, 1), (3, 1), (2, 0), (2, 1))
CHUNK = 64
LOG2_E = 1.4426950408889634


def halves(row):
    return row[:, :LANES], row[:, LANES:]


def lookup(row, lanes):
    return jnp.take_along_axis(
        jnp.broadcast_to(row, lanes.shape), lanes, axis=1, mode="promise_in_bounds"
    )


def join(pair):
    return jnp.concatenate(pair, axis=1)


def step_kernel(
    n_wide, kernel_decay,
    pos_h, vol_h, field_h, weight_h, slot_h, list_h,
    out_o,
    pos_v, vol_v, field_v, weight_v, slot_v, list_v,
    pack_s, pack_r, column, gauss, acc, masked, lane_of, pick,
    halo_s, halo_r, next_s, next_r,
    edge_weight, edge_slot, edge_list, edge_field, edge_part, edge_halo,
    edge_masked, edge_lane, edge_pick, edge_now, part_s,
    load_sem, send_sem, pack_rs, halo_rs, next_rs, edge_rs,
):
    wide = lax.axis_index("wide")
    narrow = lax.axis_index("narrow")
    x_at, y_at = narrow // 2, narrow % 2
    peers = [
        (wide, lax.rem(x_at + dx, 4) * 2 + lax.rem(y_at + dy, 2)) for dx, dy in PEERS
    ]
    up = (lax.rem(wide + 1, n_wide), narrow)
    down = (lax.rem(wide + n_wide - 1, n_wide), narrow)
    near_side = 1 - wide % 2
    far_side = 1 - near_side
    is_first, is_last, is_before = wide == 0, wide == n_wide - 1, wide == n_wide - 2
    first = (0, narrow)

    barrier = pltpu.get_barrier_semaphore()
    for target in (up, down, *reversed(peers)):
        pl.semaphore_signal(barrier, inc=1, device_id=target, device_id_type=MESH)

    loads = [
        pltpu.make_async_copy(src, dst, load_sem.at[i])
        for i, (src, dst) in enumerate(
            (
                (list_h, list_v), (field_h, field_v), (pos_h, pos_v), (vol_h, vol_v),
                (slot_h, slot_v), (weight_h, weight_v),
            )
        )
    ]
    for load in loads:
        load.start()

    def listed(rows, pairs):
        low, high = halves(rows)
        lanes = pairs & (LANES - 1)
        return jnp.where(pairs >= LANES, lookup(high, lanes), lookup(low, lanes))

    def set_pick(into, lists):
        for r in range(2):
            for at in range(2):
                into[2 * r + at:2 * r + at + 1] = lists[r:r + 1, at * LANES:(at + 1) * LANES]
        into[4:8] = jnp.zeros((4, LANES), jnp.int32)

    def set_stencil(masked_ref, lane_ref, slots, weights):
        lane_ref[...] = slots & (LANES - 1)
        rows_of = slots >> 7
        for h in range(6):
            masked_ref[h // 2, h % 2] = jnp.where(rows_of == h, weights, 0.0)

    def to_halo(rows, turn):
        halo_s[turn] = listed(rows, pick[...])[:4]

    def start_halo(turn):
        copies = halo_copies(turn)
        copies[1].start()
        if turn == 0:
            copies[0].start()
        else:
            @pl.when(jnp.logical_not(is_last))
            def _():
                copies[0].start()

    def edge_copy(i, src, dst):
        return pltpu.make_async_remote_copy(
            src_ref=src,
            dst_ref=dst,
            send_sem=send_sem.at[3],
            recv_sem=edge_rs.at[i],
            device_id=first,
            device_id_type=MESH,
        )

    edge_copies = [
        edge_copy(i, src, dst)
        for i, (src, dst) in enumerate(
            (
                (list_v, edge_list), (field_v, edge_field), (slot_v, edge_slot),
                (weight_v, edge_weight), (part_s, edge_part), (halo_s.at[1], edge_halo),
            )
        )
    ]

    def halo_copies(turn):
        return [
            pltpu.make_async_remote_copy(
                src_ref=halo_s.at[turn],
                dst_ref=halo_r.at[turn, side],
                send_sem=send_sem.at[1],
                recv_sem=halo_rs.at[turn, side],
                device_id=target,
                device_id_type=MESH,
            )
            for side, target in enumerate((up, down))
        ]

    def halo_wait(turn, side):
        pltpu.make_async_remote_copy(
            src_ref=halo_s.at[turn],
            dst_ref=halo_r.at[turn, side],
            send_sem=send_sem.at[1],
            recv_sem=halo_rs.at[turn, side],
            device_id=up,
            device_id_type=MESH,
        ).wait_recv()

    def lap_part(rows, kind, field_row, lane_ref=lane_of, masked_ref=masked):
        field_halves = halves(field_row)
        parts = []
        for at in range(2):
            lanes = lane_ref[:, at * LANES:(at + 1) * LANES]
            total = None
            for h, row in enumerate(rows):
                weights = masked_ref[kind, h, :, at * LANES:(at + 1) * LANES]
                term = weights * (lookup(row, lanes) - field_halves[at])
                total = term if total is None else total + term
            parts.append(jnp.sum(total.reshape(8, 8, LANES), axis=0))
        return parts

    def lap_side(turn, side, field_row):
        rows = halo_r[turn, side]
        is_high = side == 1
        rows = [jnp.where(is_high, rows[2 + h:3 + h], rows[h:h + 1]) for h in range(2)]
        return lap_part(rows, 1 + side, field_row)

    def add(*lists):
        return [functools.reduce(jnp.add, parts) for parts in zip(*lists)]

    def add_sources(slot, source):
        rows = [halves(source[r]) for r in range(5)]
        for t in range(0, 256, CHUNK):
            span = slice(t, t + CHUNK)
            total = None
            for at in range(2):
                sx, sy, sz, sv, sf = [row[at] for row in rows]
                distance = (column[0, span] - sx) ** 2
                distance = distance + (column[1, span] - sy) ** 2
                distance = distance + (column[2, span] - sz) ** 2
                value = jnp.exp2(distance * (-kernel_decay * LOG2_E)) * sv
                gauss[slot, at, span] = value
                term = value * (column[3, span] - sf)
                total = term if total is None else total + term
            if slot == 7:
                acc[span] = total
            else:
                acc[span] += total

    def add_field(slot, row):
        low, high = halves(row)
        for t in range(0, 256, CHUNK):
            span = slice(t, t + CHUNK)
            value = gauss[slot, 0, span] * low + gauss[slot, 1, span] * high
            if slot == 7:
                acc[span] = value
            else:
                acc[span] += value

    def fold(total):
        return [
            jnp.sum(total[at * LANES:(at + 1) * LANES].T.reshape(16, 8, LANES), axis=0)
            for at in range(2)
        ]

    def finish(parts):
        return join([jnp.sum(part, axis=0, keepdims=True) for part in parts])

    loads[0].wait()
    loads[1].wait()
    set_pick(pick, list_v[...])
    field = field_v[...]
    to_halo(field, 0)
    loads[2].wait()
    loads[3].wait()
    for r in range(3):
        pack_s[r] = pos_v[r:r + 1]
    pack_s[3] = vol_v[...]
    pack_s[4] = field

    pl.semaphore_wait(barrier, 2 + len(peers))

    pack_copies = [
        pltpu.make_async_remote_copy(
            src_ref=pack_s,
            dst_ref=pack_r.at[i],
            send_sem=send_sem.at[0],
            recv_sem=pack_rs.at[i],
            device_id=target,
            device_id_type=MESH,
        )
        for i, target in enumerate(peers)
    ]
    next_copies = [
        pltpu.make_async_remote_copy(
            src_ref=next_s,
            dst_ref=next_r.at[i],
            send_sem=send_sem.at[2],
            recv_sem=next_rs.at[i],
            device_id=target,
            device_id_type=MESH,
        )
        for i, target in enumerate(peers)
    ]
    for copy in reversed(pack_copies):
        copy.start()
    start_halo(0)
    loads[4].wait()
    loads[5].wait()

    @pl.when(is_last)
    def _():
        for i in range(4):
            edge_copies[i].start()

    for r, row in enumerate((pos_v[0:1], pos_v[1:2], pos_v[2:3], field)):
        for at, part in enumerate(halves(row)):
            column[r, at * LANES:(at + 1) * LANES] = jnp.broadcast_to(part, (LANES, LANES)).T
    add_sources(7, pack_s)
    set_stencil(masked, lane_of, slot_v[...], weight_v[...])
    lap = lap_part(halves(field), 0, field)
    for i in range(5):
        pack_copies[i].wait_recv()
        add_sources(i, pack_r.at[i])
    halo_wait(0, near_side)
    lap = add(lap, lap_side(0, near_side, field))
    for i in range(5, 7):
        pack_copies[i].wait_recv()
        add_sources(i, pack_r.at[i])
    part = field * field * field - field + finish(
        [kernel_strength * a - gradient_energy * b for a, b in zip(fold(acc[...]), lap)]
    )

    @pl.when(is_last)
    def _():
        part_s[...] = part
        edge_copies[4].start()

    halo_wait(0, far_side)
    now = part - gradient_energy * finish(lap_side(0, far_side, field))

    to_halo(now, 1)
    start_halo(1)

    @pl.when(is_before)
    def _():
        edge_copies[5].start()

    lap = lap_part(halves(now), 0, now)
    halo_wait(1, near_side)
    lap = add(lap, lap_side(1, near_side, now))
    for t in range(0, 256, CHUNK):
        span = slice(t, t + CHUNK)
        total = gauss[0, 0, span] + gauss[0, 1, span]
        for slot in range(1, 8):
            total = total + (gauss[slot, 0, span] + gauss[slot, 1, span])
        acc[span] = total
    mass = finish([kernel_strength * a for a in fold(acc[...])])

    @pl.when(jnp.logical_not(is_first))
    def _():
        halo_wait(1, far_side)

    @pl.when(is_first)
    def _():
        for i in range(4):
            edge_copies[i].wait_recv()
        set_pick(edge_pick, edge_list[...])
        set_stencil(edge_masked, edge_lane, edge_slot[...], edge_weight[...])
        theirs = edge_field[...]
        rows = [halo_s[0, 2 + h:3 + h] for h in range(2)]
        high = finish(lap_part(rows, 2, theirs, edge_lane, edge_masked))
        edge_copies[4].wait_recv()
        theirs_now = edge_part[...] - gradient_energy * high
        edge_now[...] = theirs_now
        halo_r[1, 0] = listed(theirs_now, edge_pick[...])[:4]

    after = field + time_step * finish(add(lap, lap_side(1, far_side, now)))

    next_s[...] = after
    for copy in reversed(next_copies):
        copy.start()
    to_halo(after, 2)
    start_halo(2)
    out_o[0] = after
    rest = after * after * after - after + mass * after
    lap = lap_part(halves(after), 0, after)
    add_field(7, after)

    @pl.when(is_first)
    def _():
        theirs_now = edge_now[...]
        edge_copies[5].wait_recv()
        rows = [
            halves(theirs_now),
            [edge_halo[h:h + 1] for h in range(2)],
            [halo_s[1, 2 + h:3 + h] for h in range(2)],
        ]
        lap_next = add(*(
            lap_part(pair, kind, theirs_now, edge_lane, edge_masked)
            for kind, pair in enumerate(rows)
        ))
        theirs_after = edge_field[...] + time_step * finish(lap_next)
        halo_r[2, 0] = listed(theirs_after, edge_pick[...])[:4]

    for i in range(3):
        next_copies[i].wait_recv()
        add_field(i, next_r[i])
    halo_wait(2, near_side)
    lap = add(lap, lap_side(2, near_side, after))
    for i in range(3, 6):
        next_copies[i].wait_recv()
        add_field(i, next_r[i])

    @pl.when(jnp.logical_not(is_first))
    def _():
        halo_wait(2, far_side)

    lap = add(lap, lap_side(2, far_side, after))
    next_copies[6].wait_recv()
    add_field(6, next_r[6])
    smooth = fold(acc[...])
    out_o[1] = rest - finish(
        [kernel_strength * a + gradient_energy * b for a, b in zip(smooth, lap)]
    )

    def sent(kind, *wholes):
        for whole in wholes:
            pltpu.make_async_copy(whole, whole, send_sem.at[kind]).wait()

    sent(0, pack_r)
    sent(1, halo_r.at[pl.ds(0, 2)])
    sent(2, next_r)

    @pl.when(jnp.logical_not(is_last))
    def _():
        sent(1, halo_r.at[2])

    @pl.when(is_last)
    def _():
        sent(3, list_v, field_v, slot_v, weight_v, part_s)

    @pl.when(is_before)
    def _():
        sent(3, halo_s.at[1])


def shards(n_wide, positions, volumes, phase_field, stencil_weights, stencil_slots, send_lists):
    own = phase_field.shape[0]
    patch_len = own * lax.axis_size("narrow")
    kernel_decay = 0.5 * float(patch_len) ** (2.0 / 3.0)
    in_hbm = pl.BlockSpec(memory_space=pltpu.HBM)
    in_vmem = pl.BlockSpec(memory_space=pltpu.VMEM)
    f32 = jnp.float32
    n_peers = len(PEERS)
    both = pl.pallas_call(
        functools.partial(step_kernel, n_wide, kernel_decay),
        out_shape=jax.ShapeDtypeStruct((2, 1, own), f32),
        in_specs=[in_hbm] * 6,
        out_specs=in_vmem,
        scratch_shapes=[
            pltpu.VMEM((3, own), f32),
            pltpu.VMEM((1, own), f32),
            pltpu.VMEM((1, own), f32),
            pltpu.VMEM(stencil_weights.shape, f32),
            pltpu.VMEM(stencil_slots.shape, jnp.int32),
            pltpu.VMEM((2, own), jnp.int32),
            pltpu.VMEM((5, 1, own), f32),
            pltpu.VMEM((n_peers, 5, 1, own), f32),
            pltpu.VMEM((4, own, LANES), f32),
            pltpu.VMEM((n_peers + 1, 2, own, LANES), f32),
            pltpu.VMEM((own, LANES), f32),
            pltpu.VMEM((3, 2, *stencil_weights.shape), f32),
            pltpu.VMEM(stencil_slots.shape, jnp.int32),
            pltpu.VMEM((8, LANES), jnp.int32),
            pltpu.VMEM((3, 4, LANES), f32),
            pltpu.VMEM((3, 2, 4, LANES), f32),
            pltpu.VMEM((1, own), f32),
            pltpu.VMEM((n_peers, 1, own), f32),
            pltpu.VMEM(stencil_weights.shape, f32),
            pltpu.VMEM(stencil_slots.shape, jnp.int32),
            pltpu.VMEM((2, own), jnp.int32),
            pltpu.VMEM((1, own), f32),
            pltpu.VMEM((1, own), f32),
            pltpu.VMEM((4, LANES), f32),
            pltpu.VMEM((3, 2, *stencil_weights.shape), f32),
            pltpu.VMEM(stencil_slots.shape, jnp.int32),
            pltpu.VMEM((8, LANES), jnp.int32),
            pltpu.VMEM((1, own), f32),
            pltpu.VMEM((1, own), f32),
            pltpu.SemaphoreType.DMA((6,)),
            pltpu.SemaphoreType.DMA((4,)),
            pltpu.SemaphoreType.DMA((n_peers,)),
            pltpu.SemaphoreType.DMA((3, 2)),
            pltpu.SemaphoreType.DMA((n_peers,)),
            pltpu.SemaphoreType.DMA((6,)),
        ],
        compiler_params=pltpu.CompilerParams(
            collective_id=0, has_side_effects=True, vmem_limit_bytes=16 * 1024 * 1024
        ),
    )(
        *(
            pltpu.with_memory_space_constraint(array, pltpu.HBM)
            for array in (
                positions,
                volumes.reshape(1, own),
                phase_field.reshape(1, own),
                stencil_weights,
                stencil_slots,
                send_lists,
            )
        )
    )
    both = both.reshape(2 * own)
    return both[:own], both[own:]


def solution(mesh):
    placed = (
        P(None, ("wide", "narrow")),
        P(("wide", "narrow")),
        P(("wide", "narrow")),
        P(None, ("wide", "narrow")),
        P(None, ("wide", "narrow")),
        P(None, ("wide", "narrow")),
    )
    return jax.shard_map(
        functools.partial(shards, mesh.shape["wide"]),
        mesh=mesh,
        in_specs=placed,
        out_specs=(P(("wide", "narrow")), P(("wide", "narrow"))),
        check_vma=False,
    )
```

```python
import functools
import jax
import jax.numpy as jnp
from jax import lax
from jax.experimental import pallas as pl
from jax.experimental.pallas import tpu as pltpu
from jax.sharding import PartitionSpec as P

kernel_strength = 0.1
gradient_energy = 0.5
time_step = 0.2

LANES = 128
MESH = pl.DeviceIdType.MESH
PEERS = ((0, 1), (1, 0), (3, 0), (1, 1), (3, 1), (2, 0), (2, 1))
CHUNK = 64
LOG2_E = 1.4426950408889634


def halves(row):
    return row[:, :LANES], row[:, LANES:]


def lookup(row, lanes):
    return jnp.take_along_axis(
        jnp.broadcast_to(row, lanes.shape), lanes, axis=1, mode="promise_in_bounds"
    )


def join(pair):
    return jnp.concatenate(pair, axis=1)


def step_kernel(
    n_wide, kernel_decay,
    pos_h, vol_h, field_h, weight_h, slot_h, list_h,
    out_o,
    pos_v, vol_v, field_v, weight_v, slot_v, list_v,
    pack_s, pack_r, column, gauss, acc, masked, lane_of, pick,
    halo_s, halo_r, next_s, next_r,
    edge_weight, edge_slot, edge_list, edge_pack, edge_halo, edge_packs,
    edge_masked, edge_lane, edge_pick, edge_now,
    load_sem, send_sem, pack_rs, halo_rs, next_rs, edge_rs, edge_packs_rs, go_sem,
):
    wide = lax.axis_index("wide")
    narrow = lax.axis_index("narrow")
    x_at, y_at = narrow // 2, narrow % 2
    peers = [
        (wide, lax.rem(x_at + dx, 4) * 2 + lax.rem(y_at + dy, 2)) for dx, dy in PEERS
    ]
    up = (lax.rem(wide + 1, n_wide), narrow)
    down = (lax.rem(wide + n_wide - 1, n_wide), narrow)
    near_side = 1 - wide % 2
    far_side = 1 - near_side
    is_first, is_last, is_before = wide == 0, wide == n_wide - 1, wide == n_wide - 2
    first = (0, narrow)

    barrier = pltpu.get_barrier_semaphore()
    greeted = wide - jnp.where(is_last, 1, 0)
    for _, at in reversed(peers):
        pl.semaphore_signal(barrier, inc=1, device_id=(greeted, at), device_id_type=MESH)
    pl.semaphore_signal(barrier, inc=1, device_id=down, device_id_type=MESH)

    @pl.when(jnp.logical_not(is_last))
    def _():
        pl.semaphore_signal(barrier, inc=1, device_id=up, device_id_type=MESH)

    loads = [
        pltpu.make_async_copy(src, dst, load_sem.at[i])
        for i, (src, dst) in enumerate(
            (
                (list_h, list_v), (field_h, field_v), (pos_h, pos_v), (vol_h, vol_v),
                (slot_h, slot_v), (weight_h, weight_v),
            )
        )
    ]
    for load in loads:
        load.start()

    def listed(rows, pairs):
        low, high = halves(rows)
        lanes = pairs & (LANES - 1)
        return jnp.where(pairs >= LANES, lookup(high, lanes), lookup(low, lanes))

    def set_pick(into, lists):
        for r in range(2):
            for at in range(2):
                into[2 * r + at:2 * r + at + 1] = lists[r:r + 1, at * LANES:(at + 1) * LANES]
        into[4:8] = jnp.zeros((4, LANES), jnp.int32)

    def set_stencil(masked_ref, lane_ref, slots, weights):
        lane_ref[...] = slots & (LANES - 1)
        rows_of = slots >> 7
        for h in range(6):
            masked_ref[h // 2, h % 2] = jnp.where(rows_of == h, weights, 0.0)

    def to_halo(rows, turn):
        halo_s[turn] = listed(rows, pick[...])[:4]

    def start_halo(turn):
        up_copy, down_copy = halo_copies(turn)
        if turn == 0:
            up_copy.start()

            @pl.when(jnp.logical_not(is_first))
            def _():
                down_copy.start()
        else:
            down_copy.start()

            @pl.when(jnp.logical_not(is_last))
            def _():
                up_copy.start()

    def edge_copy(i, src, dst):
        return pltpu.make_async_remote_copy(
            src_ref=src,
            dst_ref=dst,
            send_sem=send_sem.at[3],
            recv_sem=edge_rs.at[i],
            device_id=first,
            device_id_type=MESH,
        )

    edge_copies = [
        edge_copy(i, src, dst)
        for i, (src, dst) in enumerate(
            (
                (pack_s, edge_pack), (list_v, edge_list), (slot_v, edge_slot),
                (weight_v, edge_weight), (halo_s.at[0], edge_halo.at[0]),
                (halo_s.at[1], edge_halo.at[1]),
            )
        )
    ]

    def halo_copies(turn):
        return [
            pltpu.make_async_remote_copy(
                src_ref=halo_s.at[turn],
                dst_ref=halo_r.at[turn, side],
                send_sem=send_sem.at[1],
                recv_sem=halo_rs.at[turn, side],
                device_id=target,
                device_id_type=MESH,
            )
            for side, target in enumerate((up, down))
        ]

    def halo_wait(turn, side):
        pltpu.make_async_remote_copy(
            src_ref=halo_s.at[turn],
            dst_ref=halo_r.at[turn, side],
            send_sem=send_sem.at[1],
            recv_sem=halo_rs.at[turn, side],
            device_id=up,
            device_id_type=MESH,
        ).wait_recv()

    def lap_part(rows, kind, field_row, lane_ref=lane_of, masked_ref=masked):
        field_halves = halves(field_row)
        parts = []
        for at in range(2):
            lanes = lane_ref[:, at * LANES:(at + 1) * LANES]
            total = None
            for h, row in enumerate(rows):
                weights = masked_ref[kind, h, :, at * LANES:(at + 1) * LANES]
                term = weights * (lookup(row, lanes) - field_halves[at])
                total = term if total is None else total + term
            parts.append(jnp.sum(total.reshape(8, 8, LANES), axis=0))
        return parts

    def lap_side(turn, side, field_row):
        rows = halo_r[turn, side]
        is_high = side == 1
        rows = [jnp.where(is_high, rows[2 + h:3 + h], rows[h:h + 1]) for h in range(2)]
        return lap_part(rows, 1 + side, field_row)

    def add(*lists):
        return [functools.reduce(jnp.add, parts) for parts in zip(*lists)]

    def edge_lap(turn, rows):
        pairs = (
            halves(rows),
            [edge_halo[turn, h:h + 1] for h in range(2)],
            [halo_s[turn, 2 + h:3 + h] for h in range(2)],
        )
        return add(*(
            lap_part(pair, kind, rows, edge_lane, edge_masked) for kind, pair in enumerate(pairs)
        ))

    def add_sources(slot, source, keep=True):
        rows = [halves(source[r]) for r in range(5)]
        for t in range(0, 256, CHUNK):
            span = slice(t, t + CHUNK)
            total = None
            for at in range(2):
                sx, sy, sz, sv, sf = [row[at] for row in rows]
                distance = (column[0, span] - sx) ** 2
                distance = distance + (column[1, span] - sy) ** 2
                distance = distance + (column[2, span] - sz) ** 2
                value = jnp.exp2(distance * (-kernel_decay * LOG2_E)) * sv
                if keep:
                    gauss[slot, at, span] = value
                term = value * (column[3, span] - sf)
                total = term if total is None else total + term
            if slot == 7:
                acc[span] = total
            else:
                acc[span] += total

    def add_field(slot, row):
        low, high = halves(row)
        for t in range(0, 256, CHUNK):
            span = slice(t, t + CHUNK)
            value = gauss[slot, 0, span] * low + gauss[slot, 1, span] * high
            if slot == 7:
                acc[span] = value
            else:
                acc[span] += value

    def fold(total):
        return [
            jnp.sum(total[at * LANES:(at + 1) * LANES].T.reshape(16, 8, LANES), axis=0)
            for at in range(2)
        ]

    def finish(parts):
        return join([jnp.sum(part, axis=0, keepdims=True) for part in parts])

    loads[0].wait()
    loads[1].wait()
    set_pick(pick, list_v[...])
    field = field_v[...]
    to_halo(field, 0)
    loads[2].wait()
    loads[3].wait()
    for r in range(3):
        pack_s[r] = pos_v[r:r + 1]
    pack_s[3] = vol_v[...]
    pack_s[4] = field

    n_peers = len(peers)
    greetings = jnp.where(
        is_last, 2, jnp.where(is_before, 2 + 2 * n_peers, jnp.where(is_first, 1, 2) + n_peers)
    )
    pl.semaphore_wait(barrier, greetings)

    @pl.when(is_before)
    def _():
        pl.semaphore_signal(go_sem, inc=1, device_id=up, device_id_type=MESH)

    pack_copies = [
        pltpu.make_async_remote_copy(
            src_ref=pack_s,
            dst_ref=pack_r.at[i],
            send_sem=send_sem.at[0],
            recv_sem=pack_rs.at[i],
            device_id=target,
            device_id_type=MESH,
        )
        for i, target in enumerate(peers)
    ]
    next_copies = [
        pltpu.make_async_remote_copy(
            src_ref=next_s,
            dst_ref=next_r.at[i],
            send_sem=send_sem.at[2],
            recv_sem=next_rs.at[i],
            device_id=target,
            device_id_type=MESH,
        )
        for i, target in enumerate(peers)
    ]
    edge_pack_copies = [
        pltpu.make_async_remote_copy(
            src_ref=edge_pack,
            dst_ref=edge_packs.at[i],
            send_sem=send_sem.at[3],
            recv_sem=edge_packs_rs.at[i],
            device_id=target,
            device_id_type=MESH,
        )
        for i, target in enumerate(peers)
    ]

    @pl.when(is_last)
    def _():
        edge_copies[0].start()

    @pl.when(is_last)
    def _():
        start_halo(0)
        edge_copies[1].start()
        loads[4].wait()
        edge_copies[2].start()
        loads[5].wait()
        edge_copies[3].start()
        pl.semaphore_wait(go_sem, 1)

    for copy in reversed(pack_copies):
        copy.start()

    @pl.when(jnp.logical_not(is_last))
    def _():
        start_halo(0)

        @pl.when(is_before)
        def _():
            halo_wait(0, 1)
            edge_copies[4].start()

        loads[4].wait()
        loads[5].wait()

    def set_column(source):
        for r, row in enumerate((source[0], source[1], source[2], source[4])):
            for at, part in enumerate(halves(row)):
                span = slice(at * LANES, (at + 1) * LANES)
                column[r, span] = jnp.broadcast_to(part, (LANES, LANES)).T

    set_column(pack_s)
    add_sources(7, pack_s)
    set_stencil(masked, lane_of, slot_v[...], weight_v[...])
    lap = lap_part(halves(field), 0, field)
    for i in range(5):
        pack_copies[i].wait_recv()
        add_sources(i, pack_r.at[i])

    @pl.when(jnp.logical_not(is_before))
    def _():
        halo_wait(0, near_side)

    lap = add(lap, lap_side(0, near_side, field))
    for i in range(5, 7):
        pack_copies[i].wait_recv()
        add_sources(i, pack_r.at[i])
    part = field * field * field - field + finish(
        [kernel_strength * a - gradient_energy * b for a, b in zip(fold(acc[...]), lap)]
    )

    @pl.when(is_first)
    def _():
        edge_copies[0].wait_recv()
        for copy in reversed(edge_pack_copies):
            copy.start()

    halo_wait(0, far_side)

    @pl.when(is_first)
    def _():
        _, down_copy = halo_copies(0)
        down_copy.start()

    now = part - gradient_energy * finish(lap_side(0, far_side, field))

    to_halo(now, 1)
    start_halo(1)

    @pl.when(is_before)
    def _():
        edge_copies[5].start()

    lap = lap_part(halves(now), 0, now)
    halo_wait(1, near_side)
    lap = add(lap, lap_side(1, near_side, now))
    for t in range(0, 256, CHUNK):
        span = slice(t, t + CHUNK)
        total = gauss[0, 0, span] + gauss[0, 1, span]
        for slot in range(1, 8):
            total = total + (gauss[slot, 0, span] + gauss[slot, 1, span])
        acc[span] = total
    mass = finish([kernel_strength * a for a in fold(acc[...])])

    @pl.when(jnp.logical_not(is_first))
    def _():
        halo_wait(1, far_side)

    @pl.when(is_first)
    def _():
        set_column(edge_pack)
        add_sources(7, edge_pack, keep=False)
        for i in range(3):
            edge_pack_copies[i].wait_recv()
            add_sources(i, edge_packs.at[i], keep=False)
        for i in range(1, 5):
            edge_copies[i].wait_recv()
        set_pick(edge_pick, edge_list[...])
        set_stencil(edge_masked, edge_lane, edge_slot[...], edge_weight[...])
        theirs = edge_pack[4]
        their_lap = edge_lap(0, theirs)
        for i in range(3, n_peers):
            edge_pack_copies[i].wait_recv()
            add_sources(i, edge_packs.at[i], keep=False)
        theirs_now = theirs * theirs * theirs - theirs + finish(
            [
                kernel_strength * a - gradient_energy * b
                for a, b in zip(fold(acc[...]), their_lap)
            ]
        )
        edge_now[...] = theirs_now
        halo_r[1, 0] = listed(theirs_now, edge_pick[...])[:4]

    after = field + time_step * finish(add(lap, lap_side(1, far_side, now)))

    next_s[...] = after
    for copy in reversed(next_copies):
        copy.start()
    to_halo(after, 2)
    start_halo(2)
    out_o[0] = after
    rest = after * after * after - after + mass * after
    lap = lap_part(halves(after), 0, after)
    add_field(7, after)

    @pl.when(is_first)
    def _():
        theirs_now = edge_now[...]
        edge_copies[5].wait_recv()
        theirs_after = edge_pack[4] + time_step * finish(edge_lap(1, theirs_now))
        halo_r[2, 0] = listed(theirs_after, edge_pick[...])[:4]

    for i in range(3):
        next_copies[i].wait_recv()
        add_field(i, next_r[i])
    halo_wait(2, near_side)
    lap = add(lap, lap_side(2, near_side, after))
    for i in range(3, 6):
        next_copies[i].wait_recv()
        add_field(i, next_r[i])

    @pl.when(jnp.logical_not(is_first))
    def _():
        halo_wait(2, far_side)

    lap = add(lap, lap_side(2, far_side, after))
    next_copies[6].wait_recv()
    add_field(6, next_r[6])
    smooth = fold(acc[...])
    out_o[1] = rest - finish(
        [kernel_strength * a + gradient_energy * b for a, b in zip(smooth, lap)]
    )

    def sent(kind, *wholes):
        for whole in wholes:
            pltpu.make_async_copy(whole, whole, send_sem.at[kind]).wait()

    sent(0, pack_r)
    sent(1, halo_r.at[pl.ds(0, 2)])
    sent(2, next_r)

    @pl.when(jnp.logical_not(is_last))
    def _():
        sent(1, halo_r.at[2])

    @pl.when(is_last)
    def _():
        sent(3, pack_s, list_v, slot_v, weight_v)

    @pl.when(is_before)
    def _():
        sent(3, halo_s.at[pl.ds(0, 2)])

    @pl.when(is_first)
    def _():
        sent(3, edge_packs)


def shards(n_wide, positions, volumes, phase_field, stencil_weights, stencil_slots, send_lists):
    own = phase_field.shape[0]
    patch_len = own * lax.axis_size("narrow")
    kernel_decay = 0.5 * float(patch_len) ** (2.0 / 3.0)
    in_hbm = pl.BlockSpec(memory_space=pltpu.HBM)
    in_vmem = pl.BlockSpec(memory_space=pltpu.VMEM)
    f32 = jnp.float32
    n_peers = len(PEERS)
    both = pl.pallas_call(
        functools.partial(step_kernel, n_wide, kernel_decay),
        out_shape=jax.ShapeDtypeStruct((2, 1, own), f32),
        in_specs=[in_hbm] * 6,
        out_specs=in_vmem,
        scratch_shapes=[
            pltpu.VMEM((3, own), f32),
            pltpu.VMEM((1, own), f32),
            pltpu.VMEM((1, own), f32),
            pltpu.VMEM(stencil_weights.shape, f32),
            pltpu.VMEM(stencil_slots.shape, jnp.int32),
            pltpu.VMEM((2, own), jnp.int32),
            pltpu.VMEM((5, 1, own), f32),
            pltpu.VMEM((n_peers, 5, 1, own), f32),
            pltpu.VMEM((4, own, LANES), f32),
            pltpu.VMEM((n_peers + 1, 2, own, LANES), f32),
            pltpu.VMEM((own, LANES), f32),
            pltpu.VMEM((3, 2, *stencil_weights.shape), f32),
            pltpu.VMEM(stencil_slots.shape, jnp.int32),
            pltpu.VMEM((8, LANES), jnp.int32),
            pltpu.VMEM((3, 4, LANES), f32),
            pltpu.VMEM((3, 2, 4, LANES), f32),
            pltpu.VMEM((1, own), f32),
            pltpu.VMEM((n_peers, 1, own), f32),
            pltpu.VMEM(stencil_weights.shape, f32),
            pltpu.VMEM(stencil_slots.shape, jnp.int32),
            pltpu.VMEM((2, own), jnp.int32),
            pltpu.VMEM((5, 1, own), f32),
            pltpu.VMEM((2, 4, LANES), f32),
            pltpu.VMEM((n_peers, 5, 1, own), f32),
            pltpu.VMEM((3, 2, *stencil_weights.shape), f32),
            pltpu.VMEM(stencil_slots.shape, jnp.int32),
            pltpu.VMEM((8, LANES), jnp.int32),
            pltpu.VMEM((1, own), f32),
            pltpu.SemaphoreType.DMA((6,)),
            pltpu.SemaphoreType.DMA((4,)),
            pltpu.SemaphoreType.DMA((n_peers,)),
            pltpu.SemaphoreType.DMA((3, 2)),
            pltpu.SemaphoreType.DMA((n_peers,)),
            pltpu.SemaphoreType.DMA((6,)),
            pltpu.SemaphoreType.DMA((n_peers,)),
            pltpu.SemaphoreType.REGULAR,
        ],
        compiler_params=pltpu.CompilerParams(
            collective_id=0, has_side_effects=True, vmem_limit_bytes=16 * 1024 * 1024
        ),
    )(
        *(
            pltpu.with_memory_space_constraint(array, pltpu.HBM)
            for array in (
                positions,
                volumes.reshape(1, own),
                phase_field.reshape(1, own),
                stencil_weights,
                stencil_slots,
                send_lists,
            )
        )
    )
    both = both.reshape(2 * own)
    return both[:own], both[own:]


def solution(mesh):
    placed = (
        P(None, ("wide", "narrow")),
        P(("wide", "narrow")),
        P(("wide", "narrow")),
        P(None, ("wide", "narrow")),
        P(None, ("wide", "narrow")),
        P(None, ("wide", "narrow")),
    )
    return jax.shard_map(
        functools.partial(shards, mesh.shape["wide"]),
        mesh=mesh,
        in_specs=placed,
        out_specs=(P(("wide", "narrow")), P(("wide", "narrow"))),
        check_vma=False,
    )
```

```python
import functools
import jax
import jax.numpy as jnp
from jax import lax
from jax.experimental import pallas as pl
from jax.experimental.pallas import tpu as pltpu
from jax.sharding import PartitionSpec as P

kernel_strength = 0.1
gradient_energy = 0.5
time_step = 0.2

LANES = 128
MESH = pl.DeviceIdType.MESH
PEERS = ((0, 1), (1, 0), (3, 0), (1, 1), (3, 1), (2, 0), (2, 1))
CHUNK = 64
LOG2_E = 1.4426950408889634


def halves(row):
    return row[:, :LANES], row[:, LANES:]


def lookup(row, lanes):
    return jnp.take_along_axis(
        jnp.broadcast_to(row, lanes.shape), lanes, axis=1, mode="promise_in_bounds"
    )


def join(pair):
    return jnp.concatenate(pair, axis=1)


def step_kernel(
    n_wide, kernel_decay,
    pos_h, vol_h, field_h, weight_h, slot_h, list_h,
    out_o,
    pos_v, vol_v, field_v, weight_v, slot_v, list_v,
    pack_s, pack_r, column, gauss, acc, masked, lane_of, pick,
    halo_s, halo_r, next_s, next_r,
    edge_weight, edge_slot, edge_list, edge_pos, edge_vol, edge_field, edge_pack, edge_halo, edge_packs,
    edge_masked, edge_lane, edge_pick, edge_now,
    load_sem, send_sem, pack_rs, halo_rs, next_rs, edge_rs, edge_packs_rs, go_sem,
):
    wide = lax.axis_index("wide")
    narrow = lax.axis_index("narrow")
    x_at, y_at = narrow // 2, narrow % 2
    peers = [
        (wide, lax.rem(x_at + dx, 4) * 2 + lax.rem(y_at + dy, 2)) for dx, dy in PEERS
    ]
    up = (lax.rem(wide + 1, n_wide), narrow)
    down = (lax.rem(wide + n_wide - 1, n_wide), narrow)
    near_side = 1 - wide % 2
    far_side = 1 - near_side
    is_first, is_last, is_before = wide == 0, wide == n_wide - 1, wide == n_wide - 2
    first = (0, narrow)
    before = (n_wide - 2, narrow)

    loads = [
        pltpu.make_async_copy(src, dst, load_sem.at[i])
        for i, (src, dst) in enumerate(
            (
                (list_h, list_v), (field_h, field_v), (pos_h, pos_v), (vol_h, vol_v),
                (slot_h, slot_v), (weight_h, weight_v),
            )
        )
    ]
    for load in loads:
        load.start()

    barrier = pltpu.get_barrier_semaphore()
    greeted = wide - jnp.where(is_last, 1, 0)
    for _, at in reversed(peers):
        pl.semaphore_signal(barrier, inc=1, device_id=(greeted, at), device_id_type=MESH)
    pl.semaphore_signal(barrier, inc=1, device_id=down, device_id_type=MESH)

    @pl.when(wide < n_wide - 2)
    def _():
        pl.semaphore_signal(barrier, inc=1, device_id=up, device_id_type=MESH)

    @pl.when(is_first)
    def _():
        pl.semaphore_signal(barrier, inc=1, device_id=before, device_id_type=MESH)

    def listed(rows, pairs):
        low, high = halves(rows)
        lanes = pairs & (LANES - 1)
        return jnp.where(pairs >= LANES, lookup(high, lanes), lookup(low, lanes))

    def set_pack(into, pos, vol, rows):
        for r in range(3):
            into[r] = pos[r:r + 1]
        into[3] = vol
        into[4] = rows

    def set_pick(into, lists):
        for r in range(2):
            for at in range(2):
                into[2 * r + at:2 * r + at + 1] = lists[r:r + 1, at * LANES:(at + 1) * LANES]
        into[4:8] = jnp.zeros((4, LANES), jnp.int32)

    def set_stencil(masked_ref, lane_ref, slots, weights):
        lane_ref[...] = slots & (LANES - 1)
        rows_of = slots >> 7
        for h in range(6):
            masked_ref[h // 2, h % 2] = jnp.where(rows_of == h, weights, 0.0)

    def to_halo(rows, turn):
        halo_s[turn] = listed(rows, pick[...])[:4]

    def start_halo(turn):
        up_copy, down_copy = halo_copies(turn)
        if turn == 0:
            up_copy.start()

            @pl.when(jnp.logical_not(is_first | is_last))
            def _():
                down_copy.start()
        else:
            down_copy.start()

            @pl.when(jnp.logical_not(is_last))
            def _():
                up_copy.start()

    def edge_copy(i, src, dst):
        return pltpu.make_async_remote_copy(
            src_ref=src,
            dst_ref=dst,
            send_sem=send_sem.at[3],
            recv_sem=edge_rs.at[i],
            device_id=first,
            device_id_type=MESH,
        )

    edge_copies = [
        edge_copy(i, src, dst)
        for i, (src, dst) in enumerate(
            (
                (pos_h, edge_pos), (vol_h, edge_vol), (field_h, edge_field), (list_h, edge_list),
                (slot_h, edge_slot), (weight_h, edge_weight),
                (halo_s.at[0], edge_halo.at[0]), (halo_s.at[1], edge_halo.at[1]),
            )
        )
    ]

    def halo_copies(turn):
        return [
            pltpu.make_async_remote_copy(
                src_ref=halo_s.at[turn],
                dst_ref=halo_r.at[turn, side],
                send_sem=send_sem.at[1],
                recv_sem=halo_rs.at[turn, side],
                device_id=target,
                device_id_type=MESH,
            )
            for side, target in enumerate((up, down))
        ]

    def halo_wait(turn, side):
        pltpu.make_async_remote_copy(
            src_ref=halo_s.at[turn],
            dst_ref=halo_r.at[turn, side],
            send_sem=send_sem.at[1],
            recv_sem=halo_rs.at[turn, side],
            device_id=up,
            device_id_type=MESH,
        ).wait_recv()

    def lap_part(rows, kind, field_row, lane_ref=lane_of, masked_ref=masked):
        field_halves = halves(field_row)
        parts = []
        for at in range(2):
            lanes = lane_ref[:, at * LANES:(at + 1) * LANES]
            total = None
            for h, row in enumerate(rows):
                weights = masked_ref[kind, h, :, at * LANES:(at + 1) * LANES]
                term = weights * (lookup(row, lanes) - field_halves[at])
                total = term if total is None else total + term
            parts.append(jnp.sum(total.reshape(8, 8, LANES), axis=0))
        return parts

    def lap_side(turn, side, field_row):
        rows = halo_r[turn, side]
        is_high = side == 1
        rows = [jnp.where(is_high, rows[2 + h:3 + h], rows[h:h + 1]) for h in range(2)]
        return lap_part(rows, 1 + side, field_row)

    def add(*lists):
        return [functools.reduce(jnp.add, parts) for parts in zip(*lists)]

    def edge_lap(turn, rows, kind):
        if kind == 0:
            pair = halves(rows)
        elif kind == 1:
            pair = [edge_halo[turn, h:h + 1] for h in range(2)]
        else:
            pair = [halo_s[turn, 2 + h:3 + h] for h in range(2)]
        return lap_part(pair, kind, rows, edge_lane, edge_masked)

    def add_sources(slot, source, keep=True):
        rows = [halves(source[r]) for r in range(5)]
        for t in range(0, 256, CHUNK):
            span = slice(t, t + CHUNK)
            total = None
            for at in range(2):
                sx, sy, sz, sv, sf = [row[at] for row in rows]
                distance = (column[0, span] - sx) ** 2
                distance = distance + (column[1, span] - sy) ** 2
                distance = distance + (column[2, span] - sz) ** 2
                value = jnp.exp2(distance * (-kernel_decay * LOG2_E)) * sv
                if keep:
                    gauss[slot, at, span] = value
                term = value * (column[3, span] - sf)
                total = term if total is None else total + term
            if slot == 7:
                acc[span] = total
            else:
                acc[span] += total

    def add_field(slot, row):
        low, high = halves(row)
        for t in range(0, 256, CHUNK):
            span = slice(t, t + CHUNK)
            value = gauss[slot, 0, span] * low + gauss[slot, 1, span] * high
            if slot == 7:
                acc[span] = value
            else:
                acc[span] += value

    def fold(total):
        return [
            jnp.sum(total[at * LANES:(at + 1) * LANES].T.reshape(16, 8, LANES), axis=0)
            for at in range(2)
        ]

    def finish(parts):
        return join([jnp.sum(part, axis=0, keepdims=True) for part in parts])

    @pl.when(is_last)
    def _():
        pl.semaphore_wait(barrier, 1)
        for i in range(3):
            edge_copies[i].start()

    loads[0].wait()
    loads[1].wait()
    set_pick(pick, list_v[...])
    field = field_v[...]
    to_halo(field, 0)
    loads[2].wait()
    loads[3].wait()
    set_pack(pack_s, pos_v, vol_v[...], field)

    n_peers = len(peers)
    greetings = jnp.where(is_before, 3 + 2 * n_peers, jnp.where(is_first, 1, 2) + n_peers)

    @pl.when(jnp.logical_not(is_last))
    def _():
        pl.semaphore_wait(barrier, greetings)

    @pl.when(is_before)
    def _():
        pl.semaphore_signal(go_sem, inc=1, device_id=up, device_id_type=MESH)
        edge_copies[6].start()

    pack_copies = [
        pltpu.make_async_remote_copy(
            src_ref=pack_s,
            dst_ref=pack_r.at[i],
            send_sem=send_sem.at[0],
            recv_sem=pack_rs.at[i],
            device_id=target,
            device_id_type=MESH,
        )
        for i, target in enumerate(peers)
    ]
    next_copies = [
        pltpu.make_async_remote_copy(
            src_ref=next_s,
            dst_ref=next_r.at[i],
            send_sem=send_sem.at[2],
            recv_sem=next_rs.at[i],
            device_id=target,
            device_id_type=MESH,
        )
        for i, target in enumerate(peers)
    ]
    edge_pack_copies = [
        pltpu.make_async_remote_copy(
            src_ref=edge_pack,
            dst_ref=edge_packs.at[i],
            send_sem=send_sem.at[3],
            recv_sem=edge_packs_rs.at[i],
            device_id=target,
            device_id_type=MESH,
        )
        for i, target in enumerate(peers)
    ]

    @pl.when(is_last)
    def _():
        start_halo(0)
        for i in range(3, 6):
            edge_copies[i].start()
        loads[4].wait()
        loads[5].wait()
        pl.semaphore_wait(go_sem, 1)
        halo_copies(0)[1].start()

    for copy in reversed(pack_copies):
        copy.start()

    @pl.when(jnp.logical_not(is_last))
    def _():
        start_halo(0)

        loads[4].wait()
        loads[5].wait()

    def set_column(source):
        for r, row in enumerate((source[0], source[1], source[2], source[4])):
            for at, part in enumerate(halves(row)):
                span = slice(at * LANES, (at + 1) * LANES)
                column[r, span] = jnp.broadcast_to(part, (LANES, LANES)).T

    set_column(pack_s)
    add_sources(7, pack_s)
    set_stencil(masked, lane_of, slot_v[...], weight_v[...])
    lap = lap_part(halves(field), 0, field)
    for i in range(5):
        pack_copies[i].wait_recv()
        add_sources(i, pack_r.at[i])
    halo_wait(0, near_side)
    lap = add(lap, lap_side(0, near_side, field))
    for i in range(5, 7):
        pack_copies[i].wait_recv()
        add_sources(i, pack_r.at[i])
    part = field * field * field - field + finish(
        [kernel_strength * a - gradient_energy * b for a, b in zip(fold(acc[...]), lap)]
    )

    @pl.when(is_first)
    def _():
        for i in range(3):
            edge_copies[i].wait_recv()
        set_pack(edge_pack, edge_pos, edge_vol[...], edge_field[...])
        for copy in reversed(edge_pack_copies):
            copy.start()

    halo_wait(0, far_side)

    @pl.when(is_first)
    def _():
        _, down_copy = halo_copies(0)
        down_copy.start()

    now = part - gradient_energy * finish(lap_side(0, far_side, field))

    to_halo(now, 1)
    start_halo(1)

    @pl.when(is_before)
    def _():
        edge_copies[7].start()

    lap = lap_part(halves(now), 0, now)
    halo_wait(1, near_side)
    lap = add(lap, lap_side(1, near_side, now))
    for t in range(0, 256, CHUNK):
        span = slice(t, t + CHUNK)
        total = gauss[0, 0, span] + gauss[0, 1, span]
        for slot in range(1, 8):
            total = total + (gauss[slot, 0, span] + gauss[slot, 1, span])
        acc[span] = total
    mass = finish([kernel_strength * a for a in fold(acc[...])])

    @pl.when(jnp.logical_not(is_first))
    def _():
        halo_wait(1, far_side)

    @pl.when(is_first)
    def _():
        set_column(edge_pack)
        add_sources(7, edge_pack, keep=False)
        for i in range(3):
            edge_pack_copies[i].wait_recv()
            add_sources(i, edge_packs.at[i], keep=False)
        for i in range(3, 6):
            edge_copies[i].wait_recv()
        set_pick(edge_pick, edge_list[...])
        set_stencil(edge_masked, edge_lane, edge_slot[...], edge_weight[...])
        theirs = edge_pack[4]
        their_lap = add(edge_lap(0, theirs, 0), edge_lap(0, theirs, 2))
        for i in range(3, 6):
            edge_pack_copies[i].wait_recv()
            add_sources(i, edge_packs.at[i], keep=False)
        edge_copies[6].wait_recv()
        their_lap = add(their_lap, edge_lap(0, theirs, 1))
        edge_pack_copies[6].wait_recv()
        add_sources(6, edge_packs.at[6], keep=False)
        theirs_now = theirs * theirs * theirs - theirs + finish(
            [
                kernel_strength * a - gradient_energy * b
                for a, b in zip(fold(acc[...]), their_lap)
            ]
        )
        edge_now[...] = theirs_now
        halo_r[1, 0] = listed(theirs_now, edge_pick[...])[:4]

    after = field + time_step * finish(add(lap, lap_side(1, far_side, now)))

    next_s[...] = after
    for copy in reversed(next_copies):
        copy.start()
    to_halo(after, 2)
    start_halo(2)
    out_o[0] = after
    rest = after * after * after - after + mass * after
    lap = lap_part(halves(after), 0, after)
    add_field(7, after)

    @pl.when(is_first)
    def _():
        theirs_now = edge_now[...]
        their_lap = add(edge_lap(1, theirs_now, 0), edge_lap(1, theirs_now, 2))
        edge_copies[7].wait_recv()
        their_lap = add(their_lap, edge_lap(1, theirs_now, 1))
        theirs_after = edge_pack[4] + time_step * finish(their_lap)
        halo_r[2, 0] = listed(theirs_after, edge_pick[...])[:4]

    for i in range(3):
        next_copies[i].wait_recv()
        add_field(i, next_r[i])
    halo_wait(2, near_side)
    lap = add(lap, lap_side(2, near_side, after))
    for i in range(3, 6):
        next_copies[i].wait_recv()
        add_field(i, next_r[i])

    @pl.when(jnp.logical_not(is_first))
    def _():
        halo_wait(2, far_side)

    lap = add(lap, lap_side(2, far_side, after))
    next_copies[6].wait_recv()
    add_field(6, next_r[6])
    smooth = fold(acc[...])
    out_o[1] = rest - finish(
        [kernel_strength * a + gradient_energy * b for a, b in zip(smooth, lap)]
    )

    def sent(kind, *wholes):
        for whole in wholes:
            pltpu.make_async_copy(whole, whole, send_sem.at[kind]).wait()

    sent(0, pack_r)
    sent(1, halo_r.at[pl.ds(0, 2)])
    sent(2, next_r)

    @pl.when(jnp.logical_not(is_last))
    def _():
        sent(1, halo_r.at[2])

    @pl.when(is_last)
    def _():
        sent(3, pos_v, vol_v, field_v, list_v, slot_v, weight_v)

    @pl.when(is_before)
    def _():
        sent(3, halo_s.at[pl.ds(0, 2)])

    @pl.when(is_first)
    def _():
        sent(3, edge_packs)


def shards(n_wide, positions, volumes, phase_field, stencil_weights, stencil_slots, send_lists):
    own = phase_field.shape[0]
    patch_len = own * lax.axis_size("narrow")
    kernel_decay = 0.5 * float(patch_len) ** (2.0 / 3.0)
    in_hbm = pl.BlockSpec(memory_space=pltpu.HBM)
    in_vmem = pl.BlockSpec(memory_space=pltpu.VMEM)
    f32 = jnp.float32
    n_peers = len(PEERS)
    both = pl.pallas_call(
        functools.partial(step_kernel, n_wide, kernel_decay),
        out_shape=jax.ShapeDtypeStruct((2, 1, own), f32),
        in_specs=[in_hbm] * 6,
        out_specs=in_vmem,
        scratch_shapes=[
            pltpu.VMEM((3, own), f32),
            pltpu.VMEM((1, own), f32),
            pltpu.VMEM((1, own), f32),
            pltpu.VMEM(stencil_weights.shape, f32),
            pltpu.VMEM(stencil_slots.shape, jnp.int32),
            pltpu.VMEM((2, own), jnp.int32),
            pltpu.VMEM((5, 1, own), f32),
            pltpu.VMEM((n_peers, 5, 1, own), f32),
            pltpu.VMEM((4, own, LANES), f32),
            pltpu.VMEM((n_peers + 1, 2, own, LANES), f32),
            pltpu.VMEM((own, LANES), f32),
            pltpu.VMEM((3, 2, *stencil_weights.shape), f32),
            pltpu.VMEM(stencil_slots.shape, jnp.int32),
            pltpu.VMEM((8, LANES), jnp.int32),
            pltpu.VMEM((3, 4, LANES), f32),
            pltpu.VMEM((3, 2, 4, LANES), f32),
            pltpu.VMEM((1, own), f32),
            pltpu.VMEM((n_peers, 1, own), f32),
            pltpu.VMEM(stencil_weights.shape, f32),
            pltpu.VMEM(stencil_slots.shape, jnp.int32),
            pltpu.VMEM((2, own), jnp.int32),
            pltpu.VMEM((3, own), f32),
            pltpu.VMEM((1, own), f32),
            pltpu.VMEM((1, own), f32),
            pltpu.VMEM((5, 1, own), f32),
            pltpu.VMEM((2, 4, LANES), f32),
            pltpu.VMEM((n_peers, 5, 1, own), f32),
            pltpu.VMEM((3, 2, *stencil_weights.shape), f32),
            pltpu.VMEM(stencil_slots.shape, jnp.int32),
            pltpu.VMEM((8, LANES), jnp.int32),
            pltpu.VMEM((1, own), f32),
            pltpu.SemaphoreType.DMA((6,)),
            pltpu.SemaphoreType.DMA((4,)),
            pltpu.SemaphoreType.DMA((n_peers,)),
            pltpu.SemaphoreType.DMA((3, 2)),
            pltpu.SemaphoreType.DMA((n_peers,)),
            pltpu.SemaphoreType.DMA((8,)),
            pltpu.SemaphoreType.DMA((n_peers,)),
            pltpu.SemaphoreType.REGULAR,
        ],
        compiler_params=pltpu.CompilerParams(
            collective_id=0, has_side_effects=True, vmem_limit_bytes=16 * 1024 * 1024
        ),
    )(
        *(
            pltpu.with_memory_space_constraint(array, pltpu.HBM)
            for array in (
                positions,
                volumes.reshape(1, own),
                phase_field.reshape(1, own),
                stencil_weights,
                stencil_slots,
                send_lists,
            )
        )
    )
    both = both.reshape(2 * own)
    return both[:own], both[own:]


def solution(mesh):
    placed = (
        P(None, ("wide", "narrow")),
        P(("wide", "narrow")),
        P(("wide", "narrow")),
        P(None, ("wide", "narrow")),
        P(None, ("wide", "narrow")),
        P(None, ("wide", "narrow")),
    )
    return jax.shard_map(
        functools.partial(shards, mesh.shape["wide"]),
        mesh=mesh,
        in_specs=placed,
        out_specs=(P(("wide", "narrow")), P(("wide", "narrow"))),
        check_vma=False,
    )
```

```python
import functools
import jax
import jax.numpy as jnp
from jax import lax
from jax.experimental import pallas as pl
from jax.experimental.pallas import tpu as pltpu
from jax.sharding import PartitionSpec as P

kernel_strength = 0.1
gradient_energy = 0.5
time_step = 0.2

LANES = 128
MESH = pl.DeviceIdType.MESH
PEERS = ((0, 1), (1, 0), (3, 0), (1, 1), (3, 1), (2, 0), (2, 1))
CHUNK = 128
GROUPS = (range(0, 3), range(3, 6), range(6, 7))
LOG2_E = 1.4426950408889634


def halves(row):
    return row[:, :LANES], row[:, LANES:]


def lookup(row, lanes):
    return jnp.take_along_axis(
        jnp.broadcast_to(row, lanes.shape), lanes, axis=1, mode="promise_in_bounds"
    )


def join(pair):
    return jnp.concatenate(pair, axis=1)


def await_bytes(ref, sem):
    pltpu.make_async_copy(ref, ref, sem).wait()


def step_kernel(
    n_wide, kernel_decay,
    pos_h, vol_h, field_h, weight_h, slot_h, list_h,
    out_o,
    pos_v, vol_v, field_v, weight_v, slot_v, list_v,
    pack_s, pack_r, column, gauss, acc, masked, lane_of, pick,
    halo_s, halo_r, next_s, next_r,
    edge_weight, edge_slot, edge_list, edge_pos, edge_vol, edge_field, edge_pack, edge_halo, edge_packs,
    edge_masked, edge_lane, edge_pick, edge_now,
    load_sem, send_sem, pack_rs, halo_rs, next_rs, edge_rs, edge_packs_rs, go_sem,
):
    wide = lax.axis_index("wide")
    narrow = lax.axis_index("narrow")
    x_at, y_at = narrow // 2, narrow % 2
    peers = [
        (wide, lax.rem(x_at + dx, 4) * 2 + lax.rem(y_at + dy, 2)) for dx, dy in PEERS
    ]
    up = (lax.rem(wide + 1, n_wide), narrow)
    down = (lax.rem(wide + n_wide - 1, n_wide), narrow)
    near_side = 1 - wide % 2
    far_side = 1 - near_side
    is_first, is_last, is_before = wide == 0, wide == n_wide - 1, wide == n_wide - 2
    first = (0, narrow)
    before = (n_wide - 2, narrow)

    loads = [
        pltpu.make_async_copy(src, dst, load_sem.at[kind])
        for kind, src, dst in (
            (0, list_h, list_v), (0, field_h, field_v), (0, vol_h, vol_v), (1, pos_h, pos_v),
            (2, slot_h, slot_v), (2, weight_h, weight_v),
        )
    ]
    for load in loads:
        load.start()

    barrier = pltpu.get_barrier_semaphore()
    greeted = wide - jnp.where(is_last, 1, 0)
    for _, at in reversed(peers):
        pl.semaphore_signal(barrier, inc=1, device_id=(greeted, at), device_id_type=MESH)
    pl.semaphore_signal(barrier, inc=1, device_id=down, device_id_type=MESH)

    @pl.when(wide < n_wide - 2)
    def _():
        pl.semaphore_signal(barrier, inc=1, device_id=up, device_id_type=MESH)

    @pl.when(is_first)
    def _():
        pl.semaphore_signal(barrier, inc=1, device_id=before, device_id_type=MESH)

    def listed(rows, pairs):
        low, high = halves(rows)
        lanes = pairs & (LANES - 1)
        return jnp.where(pairs >= LANES, lookup(high, lanes), lookup(low, lanes))

    def set_pack(into, pos, vol, rows):
        for r in range(3):
            into[r] = pos[r:r + 1]
        into[3] = vol
        into[4] = rows

    def set_pick(into, lists):
        for r in range(2):
            for at in range(2):
                into[2 * r + at:2 * r + at + 1] = lists[r:r + 1, at * LANES:(at + 1) * LANES]
        into[4:8] = jnp.zeros((4, LANES), jnp.int32)

    def set_stencil(masked_ref, lane_ref, slots, weights):
        lane_ref[...] = slots & (LANES - 1)
        rows_of = slots >> 7
        for h in range(6):
            masked_ref[h // 2, h % 2] = jnp.where(rows_of == h, weights, 0.0)

    def to_halo(rows, turn):
        halo_s[turn] = listed(rows, pick[...])[:4]

    def start_halo(turn):
        up_copy, down_copy = halo_copies(turn)
        if turn == 0:
            up_copy.start()

            @pl.when(jnp.logical_not(is_first | is_last))
            def _():
                down_copy.start()
        else:
            down_copy.start()

            @pl.when(jnp.logical_not(is_last))
            def _():
                up_copy.start()

    def edge_copy(i, src, dst):
        return pltpu.make_async_remote_copy(
            src_ref=src,
            dst_ref=dst,
            send_sem=send_sem,
            recv_sem=edge_rs.at[i],
            device_id=first,
            device_id_type=MESH,
        )

    edge_copies = [
        edge_copy(kind, src, dst)
        for kind, src, dst in (
            (0, pos_h, edge_pos), (1, vol_h, edge_vol), (1, field_h, edge_field),
            (1, list_h, edge_list), (2, slot_h, edge_slot), (2, weight_h, edge_weight),
            (3, halo_s.at[0], edge_halo.at[0]), (4, halo_s.at[1], edge_halo.at[1]),
        )
    ]

    def halo_copies(turn):
        return [
            pltpu.make_async_remote_copy(
                src_ref=halo_s.at[turn],
                dst_ref=halo_r.at[turn, side],
                send_sem=send_sem,
                recv_sem=halo_rs.at[turn, side],
                device_id=target,
                device_id_type=MESH,
            )
            for side, target in enumerate((up, down))
        ]

    def halo_wait(turn, side):
        pltpu.make_async_remote_copy(
            src_ref=halo_s.at[turn],
            dst_ref=halo_r.at[turn, side],
            send_sem=send_sem,
            recv_sem=halo_rs.at[turn, side],
            device_id=up,
            device_id_type=MESH,
        ).wait_recv()

    def lap_part(rows, kind, field_row, lane_ref=lane_of, masked_ref=masked):
        field_halves = halves(field_row)
        parts = []
        for at in range(2):
            lanes = lane_ref[:, at * LANES:(at + 1) * LANES]
            total = None
            for h, row in enumerate(rows):
                weights = masked_ref[kind, h, :, at * LANES:(at + 1) * LANES]
                term = weights * (lookup(row, lanes) - field_halves[at])
                total = term if total is None else total + term
            parts.append(jnp.sum(total.reshape(8, 8, LANES), axis=0))
        return parts

    def lap_side(turn, side, field_row):
        rows = halo_r[turn, side]
        is_high = side == 1
        rows = [jnp.where(is_high, rows[2 + h:3 + h], rows[h:h + 1]) for h in range(2)]
        return lap_part(rows, 1 + side, field_row)

    def add(*lists):
        return [functools.reduce(jnp.add, parts) for parts in zip(*lists)]

    def edge_lap(turn, rows, kind):
        if kind == 0:
            pair = halves(rows)
        elif kind == 1:
            pair = [edge_halo[turn, h:h + 1] for h in range(2)]
        else:
            pair = [halo_s[turn, 2 + h:3 + h] for h in range(2)]
        return lap_part(pair, kind, rows, edge_lane, edge_masked)

    def add_sources(slot, source, keep=True):
        rows = [halves(source[r]) for r in range(5)]
        for t in range(0, 256, CHUNK):
            span = slice(t, t + CHUNK)
            total = None
            for at in range(2):
                sx, sy, sz, sv, sf = [row[at] for row in rows]
                distance = (column[0, span] - sx) ** 2
                distance = distance + (column[1, span] - sy) ** 2
                distance = distance + (column[2, span] - sz) ** 2
                value = jnp.exp2(distance * (-kernel_decay * LOG2_E)) * sv
                if keep:
                    gauss[slot, at, span] = value
                term = value * (column[3, span] - sf)
                total = term if total is None else total + term
            if slot == 7:
                acc[span] = total
            else:
                acc[span] += total

    def add_field(slot, row):
        low, high = halves(row)
        for t in range(0, 256, CHUNK):
            span = slice(t, t + CHUNK)
            value = gauss[slot, 0, span] * low + gauss[slot, 1, span] * high
            if slot == 7:
                acc[span] = value
            else:
                acc[span] += value

    def fold(total):
        return [
            jnp.sum(total[at * LANES:(at + 1) * LANES].T.reshape(16, 8, LANES), axis=0)
            for at in range(2)
        ]

    def finish(parts):
        return join([jnp.sum(part, axis=0, keepdims=True) for part in parts])

    @pl.when(is_last)
    def _():
        pl.semaphore_wait(barrier, 1)
        for copy in edge_copies[:4]:
            copy.start()

    await_bytes(pack_s.at[pl.ds(0, 4)], load_sem.at[0])
    set_pick(pick, list_v[...])
    field = field_v[...]
    to_halo(field, 0)
    loads[3].wait()
    set_pack(pack_s, pos_v, vol_v[...], field)

    n_peers = len(peers)
    greetings = jnp.where(is_before, 3 + 2 * n_peers, jnp.where(is_first, 1, 2) + n_peers)

    @pl.when(jnp.logical_not(is_last))
    def _():
        pl.semaphore_wait(barrier, greetings)

    @pl.when(is_before)
    def _():
        pl.semaphore_signal(go_sem, inc=1, device_id=up, device_id_type=MESH)
        edge_copies[6].start()

    pack_copies = [
        pltpu.make_async_remote_copy(
            src_ref=pack_s,
            dst_ref=pack_r.at[i],
            send_sem=send_sem,
            recv_sem=pack_rs.at[i // 3],
            device_id=target,
            device_id_type=MESH,
        )
        for i, target in enumerate(peers)
    ]
    next_copies = [
        pltpu.make_async_remote_copy(
            src_ref=next_s,
            dst_ref=next_r.at[i],
            send_sem=send_sem,
            recv_sem=next_rs.at[i // 3],
            device_id=target,
            device_id_type=MESH,
        )
        for i, target in enumerate(peers)
    ]
    edge_pack_copies = [
        pltpu.make_async_remote_copy(
            src_ref=edge_pack,
            dst_ref=edge_packs.at[i],
            send_sem=send_sem,
            recv_sem=edge_packs_rs.at[i // 3],
            device_id=target,
            device_id_type=MESH,
        )
        for i, target in enumerate(peers)
    ]

    @pl.when(is_last)
    def _():
        start_halo(0)
        for copy in edge_copies[4:6]:
            copy.start()
        await_bytes(masked.at[0], load_sem.at[2])
        pl.semaphore_wait(go_sem, 1)
        halo_copies(0)[1].start()

    for copy in reversed(pack_copies):
        copy.start()

    @pl.when(jnp.logical_not(is_last))
    def _():
        start_halo(0)

        await_bytes(masked.at[0], load_sem.at[2])

    def set_column(source):
        for r, row in enumerate((source[0], source[1], source[2], source[4])):
            for at, part in enumerate(halves(row)):
                span = slice(at * LANES, (at + 1) * LANES)
                column[r, span] = jnp.broadcast_to(part, (LANES, LANES)).T

    set_column(pack_s)
    add_sources(7, pack_s)
    set_stencil(masked, lane_of, slot_v[...], weight_v[...])
    lap = lap_part(halves(field), 0, field)
    def of_group(group, buffer, sems):
        members = GROUPS[group]
        await_bytes(buffer.at[pl.ds(members.start, len(members))], sems.at[group])
        return members

    for group in range(2):
        for i in of_group(group, pack_r, pack_rs):
            add_sources(i, pack_r.at[i])
    halo_wait(0, near_side)
    lap = add(lap, lap_side(0, near_side, field))
    for i in of_group(2, pack_r, pack_rs):
        add_sources(i, pack_r.at[i])
    part = field * field * field - field + finish(
        [kernel_strength * a - gradient_energy * b for a, b in zip(fold(acc[...]), lap)]
    )

    @pl.when(is_first)
    def _():
        edge_copies[0].wait_recv()
        await_bytes(pack_s.at[pl.ds(0, 4)], edge_rs.at[1])
        set_pack(edge_pack, edge_pos, edge_vol[...], edge_field[...])
        for copy in reversed(edge_pack_copies):
            copy.start()

    halo_wait(0, far_side)

    @pl.when(is_first)
    def _():
        _, down_copy = halo_copies(0)
        down_copy.start()

    now = part - gradient_energy * finish(lap_side(0, far_side, field))

    to_halo(now, 1)
    start_halo(1)

    @pl.when(is_before)
    def _():
        edge_copies[7].start()

    lap = lap_part(halves(now), 0, now)
    halo_wait(1, near_side)
    lap = add(lap, lap_side(1, near_side, now))
    for t in range(0, 256, CHUNK):
        span = slice(t, t + CHUNK)
        total = gauss[0, 0, span] + gauss[0, 1, span]
        for slot in range(1, 8):
            total = total + (gauss[slot, 0, span] + gauss[slot, 1, span])
        acc[span] = total
    mass = finish([kernel_strength * a for a in fold(acc[...])])

    @pl.when(jnp.logical_not(is_first))
    def _():
        halo_wait(1, far_side)

    @pl.when(is_first)
    def _():
        set_column(edge_pack)
        add_sources(7, edge_pack, keep=False)
        for i in of_group(0, edge_packs, edge_packs_rs):
            add_sources(i, edge_packs.at[i], keep=False)
        await_bytes(edge_masked.at[0], edge_rs.at[2])
        set_pick(edge_pick, edge_list[...])
        set_stencil(edge_masked, edge_lane, edge_slot[...], edge_weight[...])
        theirs = edge_pack[4]
        their_lap = add(edge_lap(0, theirs, 0), edge_lap(0, theirs, 2))
        for i in of_group(1, edge_packs, edge_packs_rs):
            add_sources(i, edge_packs.at[i], keep=False)
        edge_copies[6].wait_recv()
        their_lap = add(their_lap, edge_lap(0, theirs, 1))
        for i in of_group(2, edge_packs, edge_packs_rs):
            add_sources(i, edge_packs.at[i], keep=False)
        theirs_now = theirs * theirs * theirs - theirs + finish(
            [
                kernel_strength * a - gradient_energy * b
                for a, b in zip(fold(acc[...]), their_lap)
            ]
        )
        edge_now[...] = theirs_now
        halo_r[1, 0] = listed(theirs_now, edge_pick[...])[:4]

    after = field + time_step * finish(add(lap, lap_side(1, far_side, now)))

    next_s[...] = after
    for copy in reversed(next_copies):
        copy.start()
    to_halo(after, 2)
    start_halo(2)
    out_o[0] = after
    rest = after * after * after - after + mass * after
    lap = lap_part(halves(after), 0, after)
    add_field(7, after)

    @pl.when(is_first)
    def _():
        theirs_now = edge_now[...]
        their_lap = add(edge_lap(1, theirs_now, 0), edge_lap(1, theirs_now, 2))
        edge_copies[7].wait_recv()
        their_lap = add(their_lap, edge_lap(1, theirs_now, 1))
        theirs_after = edge_pack[4] + time_step * finish(their_lap)
        halo_r[2, 0] = listed(theirs_after, edge_pick[...])[:4]

    for i in of_group(0, next_r, next_rs):
        add_field(i, next_r[i])
    halo_wait(2, near_side)
    lap = add(lap, lap_side(2, near_side, after))
    for i in of_group(1, next_r, next_rs):
        add_field(i, next_r[i])

    @pl.when(jnp.logical_not(is_first))
    def _():
        halo_wait(2, far_side)

    lap = add(lap, lap_side(2, far_side, after))
    for i in of_group(2, next_r, next_rs):
        add_field(i, next_r[i])
    smooth = fold(acc[...])
    out_o[1] = rest - finish(
        [kernel_strength * a + gradient_energy * b for a, b in zip(smooth, lap)]
    )

    def sent(*wholes):
        for whole in wholes:
            await_bytes(whole, send_sem)

    sent(pack_r, halo_r.at[pl.ds(0, 2)], next_r)

    @pl.when(jnp.logical_not(is_last))
    def _():
        sent(halo_r.at[2])

    @pl.when(is_last)
    def _():
        sent(pos_v, vol_v, field_v, list_v, slot_v, weight_v)

    @pl.when(is_before)
    def _():
        sent(halo_s.at[pl.ds(0, 2)])

    @pl.when(is_first)
    def _():
        sent(edge_packs)


def shards(n_wide, positions, volumes, phase_field, stencil_weights, stencil_slots, send_lists):
    own = phase_field.shape[0]
    patch_len = own * lax.axis_size("narrow")
    kernel_decay = 0.5 * float(patch_len) ** (2.0 / 3.0)
    in_hbm = pl.BlockSpec(memory_space=pltpu.HBM)
    in_vmem = pl.BlockSpec(memory_space=pltpu.VMEM)
    f32 = jnp.float32
    n_peers = len(PEERS)
    both = pl.pallas_call(
        functools.partial(step_kernel, n_wide, kernel_decay),
        out_shape=jax.ShapeDtypeStruct((2, 1, own), f32),
        in_specs=[in_hbm] * 6,
        out_specs=in_vmem,
        scratch_shapes=[
            pltpu.VMEM((3, own), f32),
            pltpu.VMEM((1, own), f32),
            pltpu.VMEM((1, own), f32),
            pltpu.VMEM(stencil_weights.shape, f32),
            pltpu.VMEM(stencil_slots.shape, jnp.int32),
            pltpu.VMEM((2, own), jnp.int32),
            pltpu.VMEM((5, 1, own), f32),
            pltpu.VMEM((n_peers, 5, 1, own), f32),
            pltpu.VMEM((4, own, LANES), f32),
            pltpu.VMEM((n_peers + 1, 2, own, LANES), f32),
            pltpu.VMEM((own, LANES), f32),
            pltpu.VMEM((3, 2, *stencil_weights.shape), f32),
            pltpu.VMEM(stencil_slots.shape, jnp.int32),
            pltpu.VMEM((8, LANES), jnp.int32),
            pltpu.VMEM((3, 4, LANES), f32),
            pltpu.VMEM((3, 2, 4, LANES), f32),
            pltpu.VMEM((1, own), f32),
            pltpu.VMEM((n_peers, 1, own), f32),
            pltpu.VMEM(stencil_weights.shape, f32),
            pltpu.VMEM(stencil_slots.shape, jnp.int32),
            pltpu.VMEM((2, own), jnp.int32),
            pltpu.VMEM((3, own), f32),
            pltpu.VMEM((1, own), f32),
            pltpu.VMEM((1, own), f32),
            pltpu.VMEM((5, 1, own), f32),
            pltpu.VMEM((2, 4, LANES), f32),
            pltpu.VMEM((n_peers, 5, 1, own), f32),
            pltpu.VMEM((3, 2, *stencil_weights.shape), f32),
            pltpu.VMEM(stencil_slots.shape, jnp.int32),
            pltpu.VMEM((8, LANES), jnp.int32),
            pltpu.VMEM((1, own), f32),
            pltpu.SemaphoreType.DMA((3,)),
            pltpu.SemaphoreType.DMA,
            pltpu.SemaphoreType.DMA((len(GROUPS),)),
            pltpu.SemaphoreType.DMA((3, 2)),
            pltpu.SemaphoreType.DMA((len(GROUPS),)),
            pltpu.SemaphoreType.DMA((5,)),
            pltpu.SemaphoreType.DMA((len(GROUPS),)),
            pltpu.SemaphoreType.REGULAR,
        ],
        compiler_params=pltpu.CompilerParams(
            collective_id=0, has_side_effects=True, vmem_limit_bytes=16 * 1024 * 1024
        ),
    )(
        *(
            pltpu.with_memory_space_constraint(array, pltpu.HBM)
            for array in (
                positions,
                volumes.reshape(1, own),
                phase_field.reshape(1, own),
                stencil_weights,
                stencil_slots,
                send_lists,
            )
        )
    )
    both = both.reshape(2 * own)
    return both[:own], both[own:]


def solution(mesh):
    placed = (
        P(None, ("wide", "narrow")),
        P(("wide", "narrow")),
        P(("wide", "narrow")),
        P(None, ("wide", "narrow")),
        P(None, ("wide", "narrow")),
        P(None, ("wide", "narrow")),
    )
    return jax.shard_map(
        functools.partial(shards, mesh.shape["wide"]),
        mesh=mesh,
        in_specs=placed,
        out_specs=(P(("wide", "narrow")), P(("wide", "narrow"))),
        check_vma=False,
    )
```

```python
import functools
import jax
import jax.numpy as jnp
from jax import lax
from jax.experimental import pallas as pl
from jax.experimental.pallas import tpu as pltpu
from jax.sharding import PartitionSpec as P

kernel_strength = 0.1
gradient_energy = 0.5
time_step = 0.2

LANES = 128
MESH = pl.DeviceIdType.MESH
PEERS = ((0, 1), (1, 0), (3, 0), (1, 1), (3, 1), (2, 0), (2, 1))
CHUNK = 128
GROUPS = (range(0, 3), range(3, 6), range(6, 7))
LOG2_E = 1.4426950408889634


def halves(row):
    return row[:, :LANES], row[:, LANES:]


def lookup(row, lanes):
    return jnp.take_along_axis(
        jnp.broadcast_to(row, lanes.shape), lanes, axis=1, mode="promise_in_bounds"
    )


def join(pair):
    return jnp.concatenate(pair, axis=1)


def await_bytes(ref, sem):
    pltpu.make_async_copy(ref, ref, sem).wait()


def step_kernel(
    n_wide, kernel_decay,
    pos_h, vol_h, field_h, weight_h, slot_h, list_h,
    out_o,
    pos_v, vol_v, field_v, weight_v, slot_v, list_v,
    pack_s, pack_r, column, gauss, acc, masked, lane_of, pick,
    halo_s, halo_r, next_s, next_r,
    edge_weight, edge_slot, edge_list, edge_pos, edge_vol, edge_field, edge_pack, edge_halo, edge_packs,
    edge_masked, edge_lane, edge_pick, edge_now,
    load_sem, send_sem, pack_rs, halo_rs, next_rs, edge_rs, edge_packs_rs, go_sem,
):
    wide = lax.axis_index("wide")
    narrow = lax.axis_index("narrow")
    x_at, y_at = narrow // 2, narrow % 2
    peers = [
        (wide, lax.rem(x_at + dx, 4) * 2 + lax.rem(y_at + dy, 2)) for dx, dy in PEERS
    ]
    up = (lax.rem(wide + 1, n_wide), narrow)
    down = (lax.rem(wide + n_wide - 1, n_wide), narrow)
    near_side = 1 - wide % 2
    far_side = 1 - near_side
    is_first, is_last, is_before = wide == 0, wide == n_wide - 1, wide == n_wide - 2
    first = (0, narrow)
    before = (n_wide - 2, narrow)

    loads = [
        pltpu.make_async_copy(src, dst, load_sem.at[kind])
        for kind, src, dst in (
            (0, list_h, list_v), (0, field_h, field_v), (0, vol_h, vol_v), (1, pos_h, pos_v),
            (2, slot_h, slot_v), (2, weight_h, weight_v),
        )
    ]
    for load in loads:
        load.start()

    barrier = pltpu.get_barrier_semaphore()
    greeted = wide - jnp.where(is_last, 1, 0)
    for _, at in reversed(peers):
        pl.semaphore_signal(barrier, inc=1, device_id=(greeted, at), device_id_type=MESH)
    pl.semaphore_signal(barrier, inc=1, device_id=down, device_id_type=MESH)

    @pl.when(wide < n_wide - 2)
    def _():
        pl.semaphore_signal(barrier, inc=1, device_id=up, device_id_type=MESH)

    @pl.when(is_first)
    def _():
        pl.semaphore_signal(barrier, inc=1, device_id=before, device_id_type=MESH)

    def listed(rows, pairs):
        low, high = halves(rows)
        lanes = pairs & (LANES - 1)
        return jnp.where(pairs >= LANES, lookup(high, lanes), lookup(low, lanes))

    def set_pack(into, pos, vol, rows):
        for r in range(3):
            into[r] = pos[r:r + 1]
        into[3] = vol
        into[4] = rows

    def set_pick(into, lists):
        for r in range(2):
            for at in range(2):
                into[2 * r + at:2 * r + at + 1] = lists[r:r + 1, at * LANES:(at + 1) * LANES]
        into[4:8] = jnp.zeros((4, LANES), jnp.int32)

    def set_stencil(masked_ref, lane_ref, slots, weights):
        lane_ref[...] = slots & (LANES - 1)
        rows_of = slots >> 7
        for h in range(6):
            masked_ref[h // 2, h % 2] = jnp.where(rows_of == h, weights, 0.0)

    def to_halo(rows, turn):
        halo_s[turn] = listed(rows, pick[...])[:4]

    def start_halo(turn):
        up_copy, down_copy = halo_copies(turn)
        if turn == 0:
            up_copy.start()

            @pl.when(jnp.logical_not(is_first | is_last))
            def _():
                down_copy.start()
        else:
            down_copy.start()

            @pl.when(jnp.logical_not(is_last))
            def _():
                up_copy.start()

    def edge_copy(i, src, dst):
        return pltpu.make_async_remote_copy(
            src_ref=src,
            dst_ref=dst,
            send_sem=send_sem,
            recv_sem=edge_rs.at[i],
            device_id=first,
            device_id_type=MESH,
        )

    edge_copies = [
        edge_copy(kind, src, dst)
        for kind, src, dst in (
            (0, pos_h, edge_pos), (1, vol_h, edge_vol), (1, field_h, edge_field),
            (1, list_h, edge_list), (2, slot_h, edge_slot), (2, weight_h, edge_weight),
            (3, halo_s.at[0], edge_halo.at[0]), (4, halo_s.at[1], edge_halo.at[1]),
        )
    ]

    def halo_copies(turn):
        return [
            pltpu.make_async_remote_copy(
                src_ref=halo_s.at[turn],
                dst_ref=halo_r.at[turn, side],
                send_sem=send_sem,
                recv_sem=halo_rs.at[turn, side],
                device_id=target,
                device_id_type=MESH,
            )
            for side, target in enumerate((up, down))
        ]

    def halo_wait(turn, side):
        pltpu.make_async_remote_copy(
            src_ref=halo_s.at[turn],
            dst_ref=halo_r.at[turn, side],
            send_sem=send_sem,
            recv_sem=halo_rs.at[turn, side],
            device_id=up,
            device_id_type=MESH,
        ).wait_recv()

    def lap_part(rows, kind, field_row, lane_ref=lane_of, masked_ref=masked):
        field_halves = halves(field_row)
        parts = []
        for at in range(2):
            lanes = lane_ref[:, at * LANES:(at + 1) * LANES]
            total = None
            for h, row in enumerate(rows):
                weights = masked_ref[kind, h, :, at * LANES:(at + 1) * LANES]
                term = weights * (lookup(row, lanes) - field_halves[at])
                total = term if total is None else total + term
            parts.append(jnp.sum(total.reshape(8, 8, LANES), axis=0))
        return parts

    def lap_side(turn, side, field_row):
        rows = halo_r[turn, side]
        is_high = side == 1
        rows = [jnp.where(is_high, rows[2 + h:3 + h], rows[h:h + 1]) for h in range(2)]
        return lap_part(rows, 1 + side, field_row)

    def add(*lists):
        return [functools.reduce(jnp.add, parts) for parts in zip(*lists)]

    def edge_lap(turn, rows, kind):
        if kind == 0:
            pair = halves(rows)
        elif kind == 1:
            pair = [edge_halo[turn, h:h + 1] for h in range(2)]
        else:
            pair = [halo_s[turn, 2 + h:3 + h] for h in range(2)]
        return lap_part(pair, kind, rows, edge_lane, edge_masked)

    def add_sources(slot, source, keep=True):
        rows = [halves(source[r]) for r in range(5)]
        for t in range(0, 256, CHUNK):
            span = slice(t, t + CHUNK)
            total = None
            for at in range(2):
                sx, sy, sz, sv, sf = [row[at] for row in rows]
                distance = (column[0, span] - sx) ** 2
                distance = distance + (column[1, span] - sy) ** 2
                distance = distance + (column[2, span] - sz) ** 2
                value = jnp.exp2(distance * (-kernel_decay * LOG2_E)) * sv
                if keep:
                    gauss[slot, at, span] = value
                term = value * (column[3, span] - sf)
                total = term if total is None else total + term
            if slot == 7:
                acc[span] = total
            else:
                acc[span] += total

    def add_field(slot, row):
        low, high = halves(row)
        for t in range(0, 256, CHUNK):
            span = slice(t, t + CHUNK)
            value = gauss[slot, 0, span] * low + gauss[slot, 1, span] * high
            if slot == 7:
                acc[span] = value
            else:
                acc[span] += value

    def fold(total):
        return [
            jnp.sum(total[at * LANES:(at + 1) * LANES].T.reshape(16, 8, LANES), axis=0)
            for at in range(2)
        ]

    def finish(parts):
        return join([jnp.sum(part, axis=0, keepdims=True) for part in parts])

    @pl.when(is_last)
    def _():
        pl.semaphore_wait(barrier, 1)
        for copy in edge_copies[:4]:
            copy.start()

    await_bytes(pack_s.at[pl.ds(0, 4)], load_sem.at[0])
    set_pick(pick, list_v[...])
    field = field_v[...]
    to_halo(field, 0)
    loads[3].wait()
    set_pack(pack_s, pos_v, vol_v[...], field)

    n_peers = len(peers)
    greetings = jnp.where(is_before, 3 + 2 * n_peers, jnp.where(is_first, 1, 2) + n_peers)

    @pl.when(jnp.logical_not(is_last))
    def _():
        pl.semaphore_wait(barrier, greetings)

    @pl.when(is_before)
    def _():
        pl.semaphore_signal(go_sem, inc=1, device_id=up, device_id_type=MESH)
        edge_copies[6].start()

    pack_copies = [
        pltpu.make_async_remote_copy(
            src_ref=pack_s,
            dst_ref=pack_r.at[i],
            send_sem=send_sem,
            recv_sem=pack_rs.at[i],
            device_id=target,
            device_id_type=MESH,
        )
        for i, target in enumerate(peers)
    ]
    next_copies = [
        pltpu.make_async_remote_copy(
            src_ref=next_s,
            dst_ref=next_r.at[i],
            send_sem=send_sem,
            recv_sem=next_rs.at[i // 3],
            device_id=target,
            device_id_type=MESH,
        )
        for i, target in enumerate(peers)
    ]
    edge_pack_copies = [
        pltpu.make_async_remote_copy(
            src_ref=edge_pack,
            dst_ref=edge_packs.at[i],
            send_sem=send_sem,
            recv_sem=edge_packs_rs.at[i],
            device_id=target,
            device_id_type=MESH,
        )
        for i, target in enumerate(peers)
    ]

    @pl.when(is_last)
    def _():
        start_halo(0)
        for copy in edge_copies[4:6]:
            copy.start()
        await_bytes(masked.at[0], load_sem.at[2])
        pl.semaphore_wait(go_sem, 1)
        halo_copies(0)[1].start()

    for copy in reversed(pack_copies):
        copy.start()

    @pl.when(jnp.logical_not(is_last))
    def _():
        start_halo(0)

        await_bytes(masked.at[0], load_sem.at[2])

    def set_column(source):
        for r, row in enumerate((source[0], source[1], source[2], source[4])):
            for at, part in enumerate(halves(row)):
                span = slice(at * LANES, (at + 1) * LANES)
                column[r, span] = jnp.broadcast_to(part, (LANES, LANES)).T

    set_column(pack_s)
    add_sources(7, pack_s)
    set_stencil(masked, lane_of, slot_v[...], weight_v[...])
    lap = lap_part(halves(field), 0, field)
    def of_group(group, buffer, sems):
        members = GROUPS[group]
        await_bytes(buffer.at[pl.ds(members.start, len(members))], sems.at[group])
        return members

    for i in range(5):
        pack_copies[i].wait_recv()
        add_sources(i, pack_r.at[i])
    halo_wait(0, near_side)
    lap = add(lap, lap_side(0, near_side, field))
    for i in range(5, 7):
        pack_copies[i].wait_recv()
        add_sources(i, pack_r.at[i])
    part = field * field * field - field + finish(
        [kernel_strength * a - gradient_energy * b for a, b in zip(fold(acc[...]), lap)]
    )

    @pl.when(is_first)
    def _():
        edge_copies[0].wait_recv()
        await_bytes(pack_s.at[pl.ds(0, 4)], edge_rs.at[1])
        set_pack(edge_pack, edge_pos, edge_vol[...], edge_field[...])
        for copy in reversed(edge_pack_copies):
            copy.start()

    halo_wait(0, far_side)

    @pl.when(is_first)
    def _():
        _, down_copy = halo_copies(0)
        down_copy.start()

    now = part - gradient_energy * finish(lap_side(0, far_side, field))

    to_halo(now, 1)
    start_halo(1)

    @pl.when(is_before)
    def _():
        edge_copies[7].start()

    lap = lap_part(halves(now), 0, now)
    halo_wait(1, near_side)
    lap = add(lap, lap_side(1, near_side, now))
    for t in range(0, 256, CHUNK):
        span = slice(t, t + CHUNK)
        total = gauss[0, 0, span] + gauss[0, 1, span]
        for slot in range(1, 8):
            total = total + (gauss[slot, 0, span] + gauss[slot, 1, span])
        acc[span] = total
    mass = finish([kernel_strength * a for a in fold(acc[...])])

    @pl.when(jnp.logical_not(is_first))
    def _():
        halo_wait(1, far_side)

    @pl.when(is_first)
    def _():
        set_column(edge_pack)
        add_sources(7, edge_pack, keep=False)
        for i in GROUPS[0]:
            edge_pack_copies[i].wait_recv()
            add_sources(i, edge_packs.at[i], keep=False)
        await_bytes(edge_masked.at[0], edge_rs.at[2])
        set_pick(edge_pick, edge_list[...])
        set_stencil(edge_masked, edge_lane, edge_slot[...], edge_weight[...])
        theirs = edge_pack[4]
        their_lap = add(edge_lap(0, theirs, 0), edge_lap(0, theirs, 2))
        for i in GROUPS[1]:
            edge_pack_copies[i].wait_recv()
            add_sources(i, edge_packs.at[i], keep=False)
        edge_copies[6].wait_recv()
        their_lap = add(their_lap, edge_lap(0, theirs, 1))
        for i in GROUPS[2]:
            edge_pack_copies[i].wait_recv()
            add_sources(i, edge_packs.at[i], keep=False)
        theirs_now = theirs * theirs * theirs - theirs + finish(
            [
                kernel_strength * a - gradient_energy * b
                for a, b in zip(fold(acc[...]), their_lap)
            ]
        )
        edge_now[...] = theirs_now
        halo_r[1, 0] = listed(theirs_now, edge_pick[...])[:4]

    after = field + time_step * finish(add(lap, lap_side(1, far_side, now)))

    next_s[...] = after
    for copy in reversed(next_copies):
        copy.start()
    to_halo(after, 2)
    start_halo(2)
    out_o[0] = after
    rest = after * after * after - after + mass * after
    lap = lap_part(halves(after), 0, after)
    add_field(7, after)

    @pl.when(is_first)
    def _():
        theirs_now = edge_now[...]
        their_lap = add(edge_lap(1, theirs_now, 0), edge_lap(1, theirs_now, 2))
        edge_copies[7].wait_recv()
        their_lap = add(their_lap, edge_lap(1, theirs_now, 1))
        theirs_after = edge_pack[4] + time_step * finish(their_lap)
        halo_r[2, 0] = listed(theirs_after, edge_pick[...])[:4]

    for i in of_group(0, next_r, next_rs):
        add_field(i, next_r[i])
    halo_wait(2, near_side)
    lap = add(lap, lap_side(2, near_side, after))
    for i in of_group(1, next_r, next_rs):
        add_field(i, next_r[i])

    @pl.when(jnp.logical_not(is_first))
    def _():
        halo_wait(2, far_side)

    lap = add(lap, lap_side(2, far_side, after))
    for i in of_group(2, next_r, next_rs):
        add_field(i, next_r[i])
    smooth = fold(acc[...])
    out_o[1] = rest - finish(
        [kernel_strength * a + gradient_energy * b for a, b in zip(smooth, lap)]
    )

    def sent(*wholes):
        for whole in wholes:
            await_bytes(whole, send_sem)

    sent(pack_r, halo_r.at[pl.ds(0, 2)], next_r)

    @pl.when(jnp.logical_not(is_last))
    def _():
        sent(halo_r.at[2])

    @pl.when(is_last)
    def _():
        sent(pos_v, vol_v, field_v, list_v, slot_v, weight_v)

    @pl.when(is_before)
    def _():
        sent(halo_s.at[pl.ds(0, 2)])

    @pl.when(is_first)
    def _():
        sent(edge_packs)


def shards(n_wide, positions, volumes, phase_field, stencil_weights, stencil_slots, send_lists):
    own = phase_field.shape[0]
    patch_len = own * lax.axis_size("narrow")
    kernel_decay = 0.5 * float(patch_len) ** (2.0 / 3.0)
    in_hbm = pl.BlockSpec(memory_space=pltpu.HBM)
    in_vmem = pl.BlockSpec(memory_space=pltpu.VMEM)
    f32 = jnp.float32
    n_peers = len(PEERS)
    both = pl.pallas_call(
        functools.partial(step_kernel, n_wide, kernel_decay),
        out_shape=jax.ShapeDtypeStruct((2, 1, own), f32),
        in_specs=[in_hbm] * 6,
        out_specs=in_vmem,
        scratch_shapes=[
            pltpu.VMEM((3, own), f32),
            pltpu.VMEM((1, own), f32),
            pltpu.VMEM((1, own), f32),
            pltpu.VMEM(stencil_weights.shape, f32),
            pltpu.VMEM(stencil_slots.shape, jnp.int32),
            pltpu.VMEM((2, own), jnp.int32),
            pltpu.VMEM((5, 1, own), f32),
            pltpu.VMEM((n_peers, 5, 1, own), f32),
            pltpu.VMEM((4, own, LANES), f32),
            pltpu.VMEM((n_peers + 1, 2, own, LANES), f32),
            pltpu.VMEM((own, LANES), f32),
            pltpu.VMEM((3, 2, *stencil_weights.shape), f32),
            pltpu.VMEM(stencil_slots.shape, jnp.int32),
            pltpu.VMEM((8, LANES), jnp.int32),
            pltpu.VMEM((3, 4, LANES), f32),
            pltpu.VMEM((3, 2, 4, LANES), f32),
            pltpu.VMEM((1, own), f32),
            pltpu.VMEM((n_peers, 1, own), f32),
            pltpu.VMEM(stencil_weights.shape, f32),
            pltpu.VMEM(stencil_slots.shape, jnp.int32),
            pltpu.VMEM((2, own), jnp.int32),
            pltpu.VMEM((3, own), f32),
            pltpu.VMEM((1, own), f32),
            pltpu.VMEM((1, own), f32),
            pltpu.VMEM((5, 1, own), f32),
            pltpu.VMEM((2, 4, LANES), f32),
            pltpu.VMEM((n_peers, 5, 1, own), f32),
            pltpu.VMEM((3, 2, *stencil_weights.shape), f32),
            pltpu.VMEM(stencil_slots.shape, jnp.int32),
            pltpu.VMEM((8, LANES), jnp.int32),
            pltpu.VMEM((1, own), f32),
            pltpu.SemaphoreType.DMA((3,)),
            pltpu.SemaphoreType.DMA,
            pltpu.SemaphoreType.DMA((n_peers,)),
            pltpu.SemaphoreType.DMA((3, 2)),
            pltpu.SemaphoreType.DMA((len(GROUPS),)),
            pltpu.SemaphoreType.DMA((5,)),
            pltpu.SemaphoreType.DMA((n_peers,)),
            pltpu.SemaphoreType.REGULAR,
        ],
        compiler_params=pltpu.CompilerParams(
            collective_id=0, has_side_effects=True, vmem_limit_bytes=16 * 1024 * 1024
        ),
    )(
        *(
            pltpu.with_memory_space_constraint(array, pltpu.HBM)
            for array in (
                positions,
                volumes.reshape(1, own),
                phase_field.reshape(1, own),
                stencil_weights,
                stencil_slots,
                send_lists,
            )
        )
    )
    both = both.reshape(2 * own)
    return both[:own], both[own:]


def solution(mesh):
    placed = (
        P(None, ("wide", "narrow")),
        P(("wide", "narrow")),
        P(("wide", "narrow")),
        P(None, ("wide", "narrow")),
        P(None, ("wide", "narrow")),
        P(None, ("wide", "narrow")),
    )
    return jax.shard_map(
        functools.partial(shards, mesh.shape["wide"]),
        mesh=mesh,
        in_specs=placed,
        out_specs=(P(("wide", "narrow")), P(("wide", "narrow"))),
        check_vma=False,
    )
```
